128 devices in a mesh: row: 8 (over y_lo, z), col: 16 (over x, y_hi, core).
Axes of the slice: x: 4, y: 4 (y_hi: 2, y_lo: 2; y = y_hi * 2 + y_lo), z: 4, core: 2. Of those that a mesh axis runs over, the one named last changes fastest.
Arguments:
- frames: float32 [512, 128, 2048], P(('row', 'col')), may hold values from -1 to 6
- class_index: int32 [128, 2048], P('row', 'col'), may hold values from 0 to 7
- surface_mask: int32 [128, 2048], P('row', 'col'), may hold values 0 or 1
- effusivity: float32 [8], replicated, may hold values from 0.5 to 2
- conductivity: float32 [8], replicated, may hold values from 0.2 to 1
Outputs:
- heat_flux: float32 [128, 2048, 512], P('row', 'col')
The draws below stay inside these ranges and needn't reach their ends.
All inputs are finite; a program needn't handle non-finite values. No bound on the sum of `surface_mask` on one device may be relied on, other than what follows from the above.
Results may differ from the reference program's by a relative error of at most 0.0003.
Values sent between devices are 32-bit elements; how exact they have to be, the bound alone decides.
No kernel may reach another device: no remote copies, remote signals or barrier semaphores. Data moves between devices by JAX's collectives and lax.ppermute only.
A program may use at most 64 MiB of HBM per device.

```python
import math
import jax
import jax.numpy as jnp
from jax import lax

FRAMES = 512
NCLASS = 8
PASSES = 3
HEIGHT = 128
WIDTH = 2048


def draw_frames(key, part):
    amp_key = jax.random.fold_in(key, 11)
    onset_key = jax.random.fold_in(key, 23)
    noise_key = jax.random.fold_in(key, 37)
    amplitude = jnp.exp(jax.random.uniform(amp_key, (HEIGHT, WIDTH), jnp.float32, math.log(0.5), math.log(5.0)))
    onset = jax.random.randint(onset_key, (HEIGHT, WIDTH), 0, FRAMES // 2).astype(jnp.float32)
    times = jnp.arange(FRAMES, dtype=jnp.float32)[:, None, None]
    elapsed = jnp.maximum(times - onset[None], 0.0)
    started = jnp.where(times >= onset[None], 1.0, 0.0)
    ramp = jnp.sqrt(elapsed / (FRAMES - onset[None]))
    noise = 0.05 * jax.random.normal(noise_key, (FRAMES, HEIGHT, WIDTH), jnp.float32)
    jump_share = 0.3
    ramp_share = 0.6
    history = amplitude[None] * (ramp_share * ramp + jump_share * started + noise)
    return jnp.clip(history, -1.0, 6.0)


def plant(array, stream_key, low, top_value):
    index_at = [jax.random.randint(jax.random.fold_in(stream_key, axis), (), 0, length) for axis, length in enumerate(array.shape)]
    longest = array.shape.index(max(array.shape))
    neighbour = index_at[:longest] + [(index_at[longest] + 1) % array.shape[longest]] + index_at[longest + 1:]
    return array.at[tuple(index_at)].set(low).at[tuple(neighbour)].set(top_value)


def setup_inputs(seed: int = 0) -> dict:
    key_of = jax.random.split(jax.random.key(seed), 6)
    frames = draw_frames(jax.random.fold_in(key_of[5], 71), 0)
    class_index = plant(jax.random.randint(key_of[1], (HEIGHT, WIDTH), 0, NCLASS), jax.random.fold_in(key_of[1], 1), 0, NCLASS - 1).astype(jnp.int32)
    surface_mask = plant((jax.random.randint(key_of[2], (HEIGHT, WIDTH), 0, 4) < 3).astype(jnp.int32), jax.random.fold_in(key_of[2], 1), 0, 1)
    effusivity = jnp.clip(jnp.exp(jax.random.uniform(key_of[3], (NCLASS,), jnp.float32, math.log(0.5), math.log(2.0))), 0.5, 2.0)
    conductivity = jnp.clip(jnp.exp(jax.random.uniform(key_of[4], (NCLASS,), jnp.float32, math.log(0.2), math.log(1.0))), 0.2, 1.0)
    return dict(frames=frames, class_index=class_index, surface_mask=surface_mask, effusivity=effusivity, conductivity=conductivity)


flux_factor = 1.1283791670955126
lateral_rate = 0.24

def weights(lagged):
    clipped = jnp.maximum(lagged, 0.0)
    return jnp.where(lagged >= 0.0, 1.0 / (jnp.sqrt(clipped) + jnp.sqrt(clipped + 1.0)), 0.0)

def kernel_from(later, earlier):
    lagged = (later[:, None] - earlier[None, :]).astype(jnp.float32)
    return weights(lagged) - weights(lagged - 1.0)

def reference(frames, class_index, surface_mask, effusivity, conductivity):
    frame_ids = jnp.arange(FRAMES, dtype=jnp.int32)
    kernel = kernel_from(frame_ids, frame_ids)
    convolved = lax.dot_general(frames, kernel, (((0,), (1,)), ((), ())), precision=lax.Precision.HIGHEST)
    maskf = surface_mask.astype(jnp.float32)
    gain = flux_factor * effusivity[class_index] * maskf
    lateral = lateral_rate * conductivity[class_index] * maskf
    heat_flux = convolved * gain[:, :, None]
    for pass_index in range(PASSES):
        padded = jnp.pad(heat_flux, ((1, 1), (1, 1), (0, 0)))
        center = padded[1:-1, 1:-1]
        laplace = padded[2:, 1:-1] + padded[:-2, 1:-1] + padded[1:-1, 2:] + padded[1:-1, :-2] - 4.0 * center
        heat_flux = center + lateral[:, :, None] * laplace
    return heat_flux
```

```python
import functools

import jax
import jax.numpy as jnp
from jax import lax
from jax.experimental import pallas as pl
from jax.experimental.pallas import tpu as pltpu
from jax.sharding import Mesh
from jax.sharding import PartitionSpec as P

PASSES = 3
LANES = 128
SUB = 8

flux_factor = 1.1283791670955126
lateral_rate = 0.24

ALL = ("row", "chip", "core")


def weights(lagged):
    clipped = jnp.maximum(lagged, 0.0)
    return jnp.where(lagged >= 0.0, 1.0 / (jnp.sqrt(clipped) + jnp.sqrt(clipped + 1.0)), 0.0)


def kernel_from(later, earlier):
    lagged = (later[:, None] - earlier[None, :]).astype(jnp.float32)
    return weights(lagged) - weights(lagged - 1.0)


def smooth_body(tiles_down, tile_rows, chips, core_ref, frame_ref, mine_ref, other_ref, out_ref, gain, lat, own, ping, pong):
    tiles_across = 2 * chips
    rows = tiles_down * tile_rows
    core = core_ref[0]

    @pl.when(pl.program_id(0) == 0)
    def _():
        for tile in range(tiles_down):
            for chip in range(chips):
                part = tile * chips + chip
                at = pl.ds(tile * tile_rows, tile_rows)
                for ref, index in ((mine_ref, 2 * chip + core), (other_ref, 2 * chip + 1 - core)):
                    gain[index, at, :] = ref[part, 0:tile_rows, :]
                    lateral = ref[part, tile_rows : 2 * tile_rows, :]
                    lat[index, at, :] = lateral
                    own[index, at, :] = 1.0 - 4.0 * lateral
        edge = jnp.zeros((tiles_across, SUB, LANES), jnp.float32)
        for buffer in (ping, pong):
            buffer[:, 0:SUB, :] = edge
            buffer[:, SUB + rows : 2 * SUB + rows, :] = edge

    lane = lax.broadcasted_iota(jnp.int32, (SUB, LANES), 1)
    first, last = lane == 0, lane == LANES - 1

    @pl.loop(0, rows // SUB)
    def _(i):
        at = pl.ds(pl.multiple_of(i * SUB, SUB), SUB)
        for c in range(tiles_across):
            ping[c, pl.ds(pl.multiple_of(i * SUB + SUB, SUB), SUB), :] = (
                frame_ref[0, at, c * LANES : (c + 1) * LANES] * gain[c, at, :]
            )

    def one_pass(source, store):
        @pl.loop(0, rows // SUB)
        def _(i):
            at = pl.ds(pl.multiple_of(i * SUB, SUB), SUB)
            zero = jnp.zeros((SUB, LANES), jnp.float32)
            center = [source[c, pl.ds(pl.multiple_of(i * SUB + SUB, SUB), SUB), :] for c in range(tiles_across)]
            right_moved = [pltpu.roll(v, 1, 1) for v in center]
            left_moved = [pltpu.roll(v, LANES - 1, 1) for v in center]
            for c in range(tiles_across):
                up = source[c, pl.ds(i * SUB + SUB - 1, SUB), :]
                down = source[c, pl.ds(i * SUB + SUB + 1, SUB), :]
                left = jnp.where(first, right_moved[c - 1] if c > 0 else zero, right_moved[c])
                right = jnp.where(last, left_moved[c + 1] if c + 1 < tiles_across else zero, left_moved[c])
                around = (up + down) + (left + right)
                store(i, c, own[c, at, :] * center[c] + lat[c, at, :] * around)

    def into(buffer):
        def store(i, c, value):
            buffer[c, pl.ds(pl.multiple_of(i * SUB + SUB, SUB), SUB), :] = value

        return store

    def deliver(i, c, value):
        steps = tile_rows // SUB
        at = pl.ds(pl.multiple_of((i % steps) * SUB, SUB), SUB)
        out_ref[(i // steps) * tiles_across + c, at, :] = value

    buffers = (ping, pong)
    for index in range(PASSES):
        target = deliver if index == PASSES - 1 else into(buffers[(index + 1) % 2])
        one_pass(buffers[index % 2], target)


def smooth(core, frames, mine, other, tiles_down, tile_rows, chips):
    count, height, width = frames.shape
    across = 2 * chips
    devices = tiles_down * across
    whole = lambda f, core: (0, 0, 0)
    return pl.pallas_call(
        functools.partial(smooth_body, tiles_down, tile_rows, chips),
        out_shape=jax.ShapeDtypeStruct((devices, count * tile_rows, LANES), jnp.float32),
        grid_spec=pltpu.PrefetchScalarGridSpec(
            num_scalar_prefetch=1,
            grid=(count,),
            in_specs=[
                pl.BlockSpec((1, height, width), lambda f, core: (f, 0, 0)),
                pl.BlockSpec(mine.shape, whole),
                pl.BlockSpec(other.shape, whole),
            ],
            out_specs=pl.BlockSpec((devices, tile_rows, LANES), lambda f, core: (0, f, 0)),
            scratch_shapes=[pltpu.VMEM((across, height, LANES), jnp.float32)] * 3
            + [pltpu.VMEM((across, height + 2 * SUB, LANES), jnp.float32)] * 2,
        ),
        compiler_params=pltpu.CompilerParams(vmem_limit_bytes=48 << 20),
        name="smooth",
    )(core, frames, mine, other)


def convolve_body(count, tile_rows, devices, x_ref, high_ref, low_ref, out_ref):
    for r in range(tile_rows):
        parts = [x_ref[pl.ds(f * tile_rows + r, devices, stride=count * tile_rows), :] for f in range(count)]
        x = jnp.concatenate(parts, axis=0).T
        high = x.astype(jnp.bfloat16)
        low = (x - high.astype(jnp.float32)).astype(jnp.bfloat16)
        dot = lambda a, b: jnp.dot(a, b, preferred_element_type=jnp.float32)
        out_ref[r] = dot(high, high_ref[...]) + (dot(high, low_ref[...]) + dot(low, high_ref[...]))


def convolve(blocks, high, low, count, tile_rows):
    devices = blocks.shape[0]
    return pl.pallas_call(
        functools.partial(convolve_body, count, tile_rows, devices),
        out_shape=jax.ShapeDtypeStruct((tile_rows, LANES, high.shape[1]), jnp.float32),
        compiler_params=pltpu.CompilerParams(vmem_limit_bytes=48 << 20),
        name="convolve",
    )(blocks.reshape(devices * count * tile_rows, LANES), high, low)


def per_device(frames, class_index, surface_mask, effusivity, conductivity):
    tiles_down, chips = lax.axis_size("row"), lax.axis_size("chip")
    tile_rows = class_index.shape[0]
    count = frames.shape[0]
    devices = tiles_down * chips * 2
    core = lax.axis_index("core")

    classes = jnp.arange(effusivity.shape[0], dtype=jnp.int32)
    matches = (class_index[:, :, None] == classes[None, None, :]).astype(jnp.float32)
    maskf = surface_mask.astype(jnp.float32)
    gain = flux_factor * jnp.sum(matches * effusivity, axis=-1) * maskf
    lateral = lateral_rate * jnp.sum(matches * conductivity, axis=-1) * maskf
    maps = jnp.concatenate([gain, lateral], axis=0)
    peers = tiles_down * chips
    mine = lax.all_to_all(
        jnp.broadcast_to(maps[None], (peers, 2 * tile_rows, LANES)), ("row", "chip"), split_axis=0, concat_axis=0, tiled=True
    )
    other = lax.ppermute(mine, "core", [(0, 1), (1, 0)])
    blocks = smooth(core[None].astype(jnp.int32), frames, mine, other, tiles_down, tile_rows, chips)

    frame_ids = jnp.arange(devices * count, dtype=jnp.int32)
    arrival = frame_ids % devices * count + frame_ids // devices
    kernel = kernel_from(frame_ids, arrival).T
    rounded = lax.reduce_precision(kernel, 8, 7)
    high, low = rounded.astype(jnp.bfloat16), (kernel - rounded).astype(jnp.bfloat16)

    received = lax.all_to_all(blocks, ALL, split_axis=0, concat_axis=0, tiled=True)
    return convolve(received, high, low, count, tile_rows)


def solution(mesh):
    cores = Mesh(mesh.devices.reshape(mesh.shape["row"], mesh.shape["col"] // 2, 2), ALL)
    tile = P("row", ("chip", "core"))
    in_specs = (P(ALL, None, None), tile, tile, P(), P())
    return jax.shard_map(
        per_device, mesh=cores, in_specs=in_specs, out_specs=P("row", ("chip", "core"), None), check_vma=False
    )
```

```python
import functools

import jax
import jax.numpy as jnp
from jax import lax
from jax.experimental import pallas as pl
from jax.experimental.pallas import tpu as pltpu
from jax.sharding import Mesh
from jax.sharding import PartitionSpec as P

PASSES = 3
LANES = 128
SUB = 8

flux_factor = 1.1283791670955126
lateral_rate = 0.24

ALL = ("row", "chip", "core")


def weights(lagged):
    clipped = jnp.maximum(lagged, 0.0)
    return jnp.where(lagged >= 0.0, 1.0 / (jnp.sqrt(clipped) + jnp.sqrt(clipped + 1.0)), 0.0)


def kernel_from(later, earlier):
    lagged = (later[:, None] - earlier[None, :]).astype(jnp.float32)
    return weights(lagged) - weights(lagged - 1.0)


def smooth_body(
    tiles_down, tile_rows, chips,
    core_ref, frames_ref, mine_ref, other_ref, out_ref,
    loaded, gain, lat, own, ping, pong, ready, load_sem, store_sem,
):
    tiles_across = 2 * chips
    count, rows, _ = frames_ref.shape
    core = core_ref[0]
    steps = rows // SUB

    def load(f):
        return pltpu.make_async_copy(frames_ref.at[f], loaded.at[f], load_sem.at[f])

    def deliver(slot, f):
        part = pl.ds(pl.multiple_of(f * tile_rows, tile_rows), tile_rows)
        return pltpu.make_async_copy(ready.at[slot], out_ref.at[:, part, :], store_sem.at[slot])

    for f in range(count):
        load(f).start()
    for tile in range(tiles_down):
        for chip in range(chips):
            part = tile * chips + chip
            at = pl.ds(tile * tile_rows, tile_rows)
            for ref, index in ((mine_ref, 2 * chip + core), (other_ref, 2 * chip + 1 - core)):
                gain[index, at, :] = ref[part, 0:tile_rows, :]
                lateral = ref[part, tile_rows : 2 * tile_rows, :]
                lat[index, at, :] = lateral
                own[index, at, :] = 1.0 - 4.0 * lateral
    zero = jnp.zeros((SUB, LANES), jnp.float32)
    for buffer in (ping, pong):
        for c in range(tiles_across):
            buffer[c, 0:SUB, :] = zero
            buffer[c, SUB + rows : 2 * SUB + rows, :] = zero

    lane = lax.broadcasted_iota(jnp.int32, (SUB, LANES), 1)
    first, last = lane == 0, lane == LANES - 1

    def one_pass(source, store):
        for half in range(0, steps, SUB):
            center, right_moved, left_moved = {}, {}, {}

            def prepare(c):
                for i in range(half, half + SUB):
                    value = source[c, SUB + i * SUB : 2 * SUB + i * SUB, :]
                    center[c, i] = value
                    right_moved[c, i] = pltpu.roll(value, 1, 1)
                    left_moved[c, i] = pltpu.roll(value, LANES - 1, 1)

            prepare(0)
            for c in range(tiles_across):
                if c + 1 < tiles_across:
                    prepare(c + 1)
                for i in range(half, half + SUB):
                    at = slice(i * SUB, i * SUB + SUB)
                    up = source[c, SUB - 1 + i * SUB : 2 * SUB - 1 + i * SUB, :]
                    down = source[c, SUB + 1 + i * SUB : 2 * SUB + 1 + i * SUB, :]
                    left = jnp.where(first, right_moved[c - 1, i] if c > 0 else zero, right_moved[c, i])
                    right = jnp.where(last, left_moved[c + 1, i] if c + 1 < tiles_across else zero, left_moved[c, i])
                    around = (up + down) + (left + right)
                    store(i, c, own[c, at, :] * center[c, i] + lat[c, at, :] * around)

    def into(buffer):
        def store(i, c, value):
            buffer[c, SUB + i * SUB : 2 * SUB + i * SUB, :] = value

        return store

    buffers = (ping, pong)

    @pl.loop(0, count)
    def _(f):
        slot = f % 2
        load(f).wait()

        @pl.when(f >= 2)
        def _():
            deliver(slot, f - 2).wait()

        for c in range(tiles_across):
            ping[c, SUB : SUB + rows, :] = loaded[f, :, c * LANES : (c + 1) * LANES] * gain[c]

        def finish(i, c, value):
            tile, part = i * SUB // tile_rows, i * SUB % tile_rows
            ready[slot, tile * tiles_across + c, part : part + SUB, :] = value

        for index in range(PASSES):
            one_pass(buffers[index % 2], finish if index == PASSES - 1 else into(buffers[(index + 1) % 2]))
        deliver(slot, f).start()

    for f in range(count - 2, count):
        deliver(f % 2, f).wait()


def smooth(core, frames, mine, other, tiles_down, tile_rows, chips):
    count, height, width = frames.shape
    across = 2 * chips
    devices = tiles_down * across
    return pl.pallas_call(
        functools.partial(smooth_body, tiles_down, tile_rows, chips),
        out_shape=jax.ShapeDtypeStruct((devices, count * tile_rows, LANES), jnp.float32),
        in_specs=[pl.BlockSpec(memory_space=pltpu.SMEM), pl.BlockSpec(memory_space=pltpu.HBM)]
        + [pl.BlockSpec(memory_space=pltpu.VMEM)] * 2,
        out_specs=pl.BlockSpec(memory_space=pltpu.HBM),
        scratch_shapes=[pltpu.VMEM((count, height, width), jnp.float32)]
        + [pltpu.VMEM((across, height, LANES), jnp.float32)] * 3
        + [pltpu.VMEM((across, height + 2 * SUB, LANES), jnp.float32)] * 2
        + [pltpu.VMEM((2, devices, tile_rows, LANES), jnp.float32)]
        + [pltpu.SemaphoreType.DMA((count,)), pltpu.SemaphoreType.DMA((2,))],
        compiler_params=pltpu.CompilerParams(vmem_limit_bytes=56 << 20),
        name="smooth",
    )(core, frames, mine, other)


def convolve_body(count, devices, x_ref, high_ref, low_ref, out_ref):
    rows, _, outputs = out_ref.shape
    flat = x_ref.reshape(devices * count * SUB, LANES)
    base = pl.program_id(0) * rows % SUB
    early = devices // 2
    high, low = [], []
    for r in range(rows):
        pieces = []
        for start in (0, early):
            for pair in range(0, count, 2):
                both = [
                    flat[pl.ds((start * count + f) * SUB + base + r, early, stride=count * SUB), :]
                    for f in (pair, pair + 1)
                ]
                pieces.append(jnp.concatenate(both, axis=0).T)
        x = jnp.concatenate(pieces, axis=1)
        top = x.astype(jnp.bfloat16)
        high.append(top)
        low.append((x - top.astype(jnp.float32)).astype(jnp.bfloat16))
    high, low = jnp.concatenate(high, axis=0), jnp.concatenate(low, axis=0)

    def product(depth, columns):
        def dot(a, b_ref):
            return jnp.dot(a[:, :depth], b_ref[:depth, columns], preferred_element_type=jnp.float32)

        result = dot(high, high_ref) + (dot(high, low_ref) + dot(low, high_ref))
        out_ref[:, :, columns] = result.reshape(rows, LANES, -1)

    half = outputs // 2
    product(half, slice(0, half))
    product(outputs, slice(half, outputs))


def convolve(blocks, high, low, count, tile_rows):
    devices = blocks.shape[0]
    frames = high.shape[1]
    step = SUB // 2
    return pl.pallas_call(
        functools.partial(convolve_body, count, devices),
        out_shape=jax.ShapeDtypeStruct((tile_rows, LANES, frames), jnp.float32),
        grid=(tile_rows // step,),
        in_specs=[
            pl.BlockSpec((devices, count, 1, SUB, LANES), lambda i: (0, 0, i * step // SUB, 0, 0)),
            pl.BlockSpec((frames, frames), lambda i: (0, 0)),
            pl.BlockSpec((frames, frames), lambda i: (0, 0)),
        ],
        out_specs=pl.BlockSpec((step, LANES, frames), lambda i: (i, 0, 0)),
        compiler_params=pltpu.CompilerParams(vmem_limit_bytes=24 << 20),
        name="convolve",
    )(blocks.reshape(devices, count, tile_rows // SUB, SUB, LANES), high, low)


def per_device(frames, class_index, surface_mask, effusivity, conductivity):
    tiles_down, chips = lax.axis_size("row"), lax.axis_size("chip")
    tile_rows = class_index.shape[0]
    count = frames.shape[0]
    devices = tiles_down * chips * 2
    core = lax.axis_index("core")

    classes = jnp.arange(effusivity.shape[0], dtype=jnp.int32)
    matches = (class_index[:, :, None] == classes[None, None, :]).astype(jnp.float32)
    maskf = surface_mask.astype(jnp.float32)
    gain = flux_factor * jnp.sum(matches * effusivity, axis=-1) * maskf
    lateral = lateral_rate * jnp.sum(matches * conductivity, axis=-1) * maskf
    maps = jnp.concatenate([gain, lateral], axis=0)
    peers = tiles_down * chips
    mine = lax.all_to_all(
        jnp.broadcast_to(maps[None], (peers, 2 * tile_rows, LANES)), ("row", "chip"), split_axis=0, concat_axis=0, tiled=True
    )
    other = lax.ppermute(mine, "core", [(0, 1), (1, 0)])
    blocks = smooth(core[None].astype(jnp.int32), frames, mine, other, tiles_down, tile_rows, chips)

    frame_ids = jnp.arange(devices * count, dtype=jnp.int32)
    early = devices // 2
    source = frame_ids // (early * count) * early + frame_ids % early
    arrival = source * count + frame_ids // early % count
    kernel = kernel_from(frame_ids, arrival).T
    rounded = lax.reduce_precision(kernel, 8, 7)
    high, low = rounded.astype(jnp.bfloat16), (kernel - rounded).astype(jnp.bfloat16)

    received = lax.all_to_all(blocks, ALL, split_axis=0, concat_axis=0, tiled=True)
    return convolve(received, high, low, count, tile_rows)


def solution(mesh):
    cores = Mesh(mesh.devices.reshape(mesh.shape["row"], mesh.shape["col"] // 2, 2), ALL)
    tile = P("row", ("chip", "core"))
    in_specs = (P(ALL, None, None), tile, tile, P(), P())
    return jax.shard_map(
        per_device, mesh=cores, in_specs=in_specs, out_specs=P("row", ("chip", "core"), None), check_vma=False
    )
```

```python
import functools

import jax
import jax.numpy as jnp
from jax import lax
from jax.experimental import pallas as pl
from jax.experimental.pallas import tpu as pltpu
from jax.sharding import Mesh
from jax.sharding import PartitionSpec as P

PASSES = 3
LANES = 128
SUB = 8
ROW_GROUP = 2

flux_factor = 1.1283791670955126
lateral_rate = 0.24

ALL = ("row", "chip", "core")


def weights(lagged):
    clipped = jnp.maximum(lagged, 0.0)
    return jnp.where(lagged >= 0.0, 1.0 / (jnp.sqrt(clipped) + jnp.sqrt(clipped + 1.0)), 0.0)


def kernel_from(later, earlier):
    lagged = (later[:, None] - earlier[None, :]).astype(jnp.float32)
    return weights(lagged) - weights(lagged - 1.0)


def smooth_body(
    tiles_down, tile_rows, chips,
    core_ref, frames_ref, mine_ref, other_ref, out_ref,
    loaded, gain, lat, own, ping, pong, ready, load_sem, store_sem,
):
    tiles_across = 2 * chips
    count, rows, _ = frames_ref.shape
    core = core_ref[0]
    steps = rows // SUB

    def load(f):
        return pltpu.make_async_copy(frames_ref.at[f], loaded.at[f], load_sem.at[f])

    def deliver(slot, f):
        part = pl.ds(pl.multiple_of(f * tile_rows, tile_rows), tile_rows)
        return pltpu.make_async_copy(ready.at[slot], out_ref.at[:, part, :], store_sem.at[slot])

    for f in range(count):
        load(f).start()
    for tile in range(tiles_down):
        for chip in range(chips):
            part = tile * chips + chip
            at = pl.ds(tile * tile_rows, tile_rows)
            for ref, index in ((mine_ref, 2 * chip + core), (other_ref, 2 * chip + 1 - core)):
                gain[index, at, :] = ref[part, 0:tile_rows, :]
                lateral = ref[part, tile_rows : 2 * tile_rows, :]
                lat[index, at, :] = lateral
                own[index, at, :] = 1.0 - 4.0 * lateral
    zero = jnp.zeros((SUB, LANES), jnp.float32)
    for buffer in (ping, pong):
        for c in range(tiles_across):
            buffer[c, 0:SUB, :] = zero
            buffer[c, SUB + rows : 2 * SUB + rows, :] = zero

    lane = lax.broadcasted_iota(jnp.int32, (SUB, LANES), 1)
    first, last = lane == 0, lane == LANES - 1

    def one_pass(source, store):
        for half in range(0, steps, SUB):
            center, right_moved, left_moved = {}, {}, {}

            def prepare(c):
                for i in range(half, half + SUB):
                    value = source[c, SUB + i * SUB : 2 * SUB + i * SUB, :]
                    center[c, i] = value
                    right_moved[c, i] = pltpu.roll(value, 1, 1)
                    left_moved[c, i] = pltpu.roll(value, LANES - 1, 1)

            prepare(0)
            for c in range(tiles_across):
                if c + 1 < tiles_across:
                    prepare(c + 1)
                for i in range(half, half + SUB):
                    at = slice(i * SUB, i * SUB + SUB)
                    up = source[c, SUB - 1 + i * SUB : 2 * SUB - 1 + i * SUB, :]
                    down = source[c, SUB + 1 + i * SUB : 2 * SUB + 1 + i * SUB, :]
                    left = jnp.where(first, right_moved[c - 1, i] if c > 0 else zero, right_moved[c, i])
                    right = jnp.where(last, left_moved[c + 1, i] if c + 1 < tiles_across else zero, left_moved[c, i])
                    around = (up + down) + (left + right)
                    store(i, c, own[c, at, :] * center[c, i] + lat[c, at, :] * around)

    def into(buffer):
        def store(i, c, value):
            buffer[c, SUB + i * SUB : 2 * SUB + i * SUB, :] = value

        return store

    buffers = (ping, pong)

    @pl.loop(0, count)
    def _(f):
        slot = f % 2
        load(f).wait()

        @pl.when(f >= 2)
        def _():
            deliver(slot, f - 2).wait()

        for c in range(tiles_across):
            ping[c, SUB : SUB + rows, :] = loaded[f, :, c * LANES : (c + 1) * LANES] * gain[c]

        def finish(i, c, value):
            tile, part = i * SUB // tile_rows, i * SUB % tile_rows
            ready[slot, tile * tiles_across + c, part : part + SUB, :] = value

        for index in range(PASSES):
            one_pass(buffers[index % 2], finish if index == PASSES - 1 else into(buffers[(index + 1) % 2]))
        deliver(slot, f).start()

    for f in range(count - 2, count):
        deliver(f % 2, f).wait()


def smooth(core, frames, mine, other, tiles_down, tile_rows, chips):
    count, height, width = frames.shape
    across = 2 * chips
    devices = tiles_down * across
    return pl.pallas_call(
        functools.partial(smooth_body, tiles_down, tile_rows, chips),
        out_shape=jax.ShapeDtypeStruct((devices, count * tile_rows, LANES), jnp.float32),
        in_specs=[pl.BlockSpec(memory_space=pltpu.SMEM), pl.BlockSpec(memory_space=pltpu.HBM)]
        + [pl.BlockSpec(memory_space=pltpu.VMEM)] * 2,
        out_specs=pl.BlockSpec(memory_space=pltpu.HBM),
        scratch_shapes=[pltpu.VMEM((count, height, width), jnp.float32)]
        + [pltpu.VMEM((across, height, LANES), jnp.float32)] * 3
        + [pltpu.VMEM((across, height + 2 * SUB, LANES), jnp.float32)] * 2
        + [pltpu.VMEM((2, devices, tile_rows, LANES), jnp.float32)]
        + [pltpu.SemaphoreType.DMA((count,)), pltpu.SemaphoreType.DMA((2,))],
        compiler_params=pltpu.CompilerParams(vmem_limit_bytes=50 << 20),
        name="smooth",
    )(core, frames, mine, other)


def convolve_body(count, rows, x_ref, high_ref, low_ref, out_ref, loaded, high, low, ready, load_sem, early_sem, late_sem):
    quarters, chunk, _ = loaded.shape
    sources = chunk // (count * rows)
    outputs = out_ref.shape[2]
    half = outputs // 2
    first, second = slice(0, half), slice(half, outputs)
    groups = rows // ROW_GROUP

    def load(q):
        return pltpu.make_async_copy(x_ref.at[pl.ds(q * chunk, chunk)], loaded.at[q], load_sem.at[q])

    def save(k, columns, sem):
        part = slice(k * ROW_GROUP, (k + 1) * ROW_GROUP)
        return pltpu.make_async_copy(ready.at[part, :, columns], out_ref.at[part, :, columns], sem.at[k])

    def prepare(q, k):
        flat = loaded.at[q]
        for r in range(k * ROW_GROUP, (k + 1) * ROW_GROUP):
            parts = [flat[pl.ds(f * rows + r, sources, stride=count * rows), :] for f in range(count)]
            x = jnp.concatenate(parts, axis=0).T
            top = x.astype(jnp.bfloat16)
            at = (slice(r * LANES, (r + 1) * LANES), slice(q * LANES, (q + 1) * LANES))
            high[at] = top
            low[at] = (x - top.astype(jnp.float32)).astype(jnp.bfloat16)

    def product(k, terms, columns):
        at = (slice(k * ROW_GROUP * LANES, (k + 1) * ROW_GROUP * LANES), terms)

        def dot(a_ref, b_ref):
            return jnp.dot(a_ref[at], b_ref[terms, columns], preferred_element_type=jnp.float32)

        result = dot(high, high_ref) + (dot(high, low_ref) + dot(low, high_ref))
        return result.reshape(ROW_GROUP, LANES, half)

    for q in range(quarters):
        load(q).start()
    load(0).wait()
    for k in range(groups):
        prepare(0, k)
    load(1).wait()
    for k in range(groups):
        part = slice(k * ROW_GROUP, (k + 1) * ROW_GROUP)
        prepare(1, k)
        ready[part, :, first] = product(k, first, first)
        save(k, first, early_sem).start()
        ready[part, :, second] = product(k, first, second)
    load(2).wait()
    load(3).wait()
    for k in range(groups):
        part = slice(k * ROW_GROUP, (k + 1) * ROW_GROUP)
        prepare(2, k)
        prepare(3, k)
        ready[part, :, second] = ready[part, :, second] + product(k, second, second)
        save(k, second, late_sem).start()
    for k in range(groups):
        save(k, first, early_sem).wait()
        save(k, second, late_sem).wait()


def convolve(blocks, high, low, count, tile_rows):
    devices = blocks.shape[0]
    frames = high.shape[1]
    quarters = 4
    return pl.pallas_call(
        functools.partial(convolve_body, count, tile_rows),
        out_shape=jax.ShapeDtypeStruct((tile_rows, LANES, frames), jnp.float32),
        in_specs=[pl.BlockSpec(memory_space=pltpu.HBM)] + [pl.BlockSpec(memory_space=pltpu.VMEM)] * 2,
        out_specs=pl.BlockSpec(memory_space=pltpu.HBM),
        scratch_shapes=[pltpu.VMEM((quarters, devices // quarters * count * tile_rows, LANES), jnp.float32)]
        + [pltpu.VMEM((tile_rows * LANES, frames), jnp.bfloat16)] * 2
        + [pltpu.VMEM((tile_rows, LANES, frames), jnp.float32)]
        + [pltpu.SemaphoreType.DMA((quarters,))]
        + [pltpu.SemaphoreType.DMA((tile_rows // ROW_GROUP,))] * 2,
        compiler_params=pltpu.CompilerParams(vmem_limit_bytes=50 << 20),
        name="convolve",
    )(blocks.reshape(devices * count * tile_rows, LANES), high, low)


def maps_body(class_ref, mask_ref, effusivity_ref, conductivity_ref, out_ref):
    classes, mask = class_ref[...], mask_ref[...].astype(jnp.float32)
    rows = classes.shape[0]
    gain = lateral = jnp.zeros_like(mask)
    for k in range(effusivity_ref.shape[0]):
        gain = jnp.where(classes == k, effusivity_ref[k], gain)
        lateral = jnp.where(classes == k, conductivity_ref[k], lateral)
    gain, lateral = flux_factor * gain * mask, lateral_rate * lateral * mask
    out_ref[0:rows, :] = gain
    out_ref[rows : 2 * rows, :] = lateral


def maps_for(class_index, surface_mask, effusivity, conductivity):
    rows = class_index.shape[0]
    return pl.pallas_call(
        maps_body,
        out_shape=jax.ShapeDtypeStruct((2 * rows, LANES), jnp.float32),
        in_specs=[pl.BlockSpec(memory_space=pltpu.VMEM)] * 2 + [pl.BlockSpec(memory_space=pltpu.SMEM)] * 2,
        out_specs=pl.BlockSpec(memory_space=pltpu.VMEM),
        name="maps",
    )(class_index, surface_mask, effusivity, conductivity)


def per_device(frames, class_index, surface_mask, effusivity, conductivity):
    tiles_down, chips = lax.axis_size("row"), lax.axis_size("chip")
    tile_rows = class_index.shape[0]
    count = frames.shape[0]
    devices = tiles_down * chips * 2
    core = lax.axis_index("core")

    maps = maps_for(class_index, surface_mask, effusivity, conductivity)
    for_all = jnp.broadcast_to(maps[None], (tiles_down * chips, *maps.shape))
    mine = lax.all_to_all(for_all, ("row", "chip"), split_axis=0, concat_axis=0, tiled=True)
    other = lax.ppermute(mine, "core", [(0, 1), (1, 0)])
    blocks = smooth(core[None].astype(jnp.int32), frames, mine, other, tiles_down, tile_rows, chips)

    frame_ids = jnp.arange(devices * count, dtype=jnp.int32)
    quarter = devices // 4
    source = frame_ids // (quarter * count) * quarter + frame_ids % quarter
    arrival = source * count + frame_ids // quarter % count
    kernel = kernel_from(frame_ids, arrival).T
    rounded = lax.reduce_precision(kernel, 8, 7)
    high, low = rounded.astype(jnp.bfloat16), (kernel - rounded).astype(jnp.bfloat16)

    received = lax.all_to_all(blocks, ALL, split_axis=0, concat_axis=0, tiled=True)
    return convolve(received, high, low, count, tile_rows)


def solution(mesh):
    cores = Mesh(mesh.devices.reshape(mesh.shape["row"], mesh.shape["col"] // 2, 2), ALL)
    tile = P("row", ("chip", "core"))
    in_specs = (P(ALL, None, None), tile, tile, P(), P())
    return jax.shard_map(
        per_device, mesh=cores, in_specs=in_specs, out_specs=P("row", ("chip", "core"), None), check_vma=False
    )
```

```python
import functools

import jax
import jax.numpy as jnp
from jax import lax
from jax.experimental import pallas as pl
from jax.experimental.pallas import tpu as pltpu
from jax.sharding import Mesh
from jax.sharding import PartitionSpec as P

LANES = 128
SUB = 8
ROW_GROUP = 2

flux_factor = 1.1283791670955126
lateral_rate = 0.24

ALL = ("row", "chip", "core")


def weights(lagged):
    clipped = jnp.maximum(lagged, 0.0)
    return jnp.where(lagged >= 0.0, 1.0 / (jnp.sqrt(clipped) + jnp.sqrt(clipped + 1.0)), 0.0)


def kernel_from(later, earlier):
    lagged = (later[:, None] - earlier[None, :]).astype(jnp.float32)
    return weights(lagged) - weights(lagged - 1.0)


def smooth_body(
    tiles_down, tile_rows, chips,
    core_ref, table_ref, frames_ref, mine_ref, other_ref, out_ref,
    loaded, gain, lat, own, ping, pong, ready, load_sem, store_sem,
):
    tiles_across = 2 * chips
    count, rows, _ = frames_ref.shape
    core = core_ref[0]
    steps = rows // SUB

    def load(f):
        return pltpu.make_async_copy(frames_ref.at[f], loaded.at[f], load_sem.at[f])

    def deliver(slot, f, half):
        part = pl.ds(pl.multiple_of(f * tile_rows, tile_rows), tile_rows)
        to = pl.ds(half * (tiles_down // 2) * tiles_across, tiles_down // 2 * tiles_across)
        return pltpu.make_async_copy(ready.at[slot, to], out_ref.at[to, part, :], store_sem.at[slot, half])

    load(0).start()
    for tile in range(tiles_down):
        for chip in range(chips):
            part = tile * chips + chip
            at = pl.ds(tile * tile_rows, tile_rows)
            for ref, index in ((mine_ref, 2 * chip + core), (other_ref, 2 * chip + 1 - core)):
                lateral = ref[part, 0:tile_rows, :]
                if ref.shape[1] == 2 * tile_rows:
                    gain[index, at, :] = ref[part, tile_rows : 2 * tile_rows, :]
                else:
                    found = jnp.zeros_like(lateral)
                    for k in range(table_ref.shape[1]):
                        found = jnp.where(lateral == table_ref[0, k], table_ref[1, k], found)
                    gain[index, at, :] = found
                lat[index, at, :] = lateral
                own[index, at, :] = 1.0 - 4.0 * lateral
    load(1).start()
    zero = jnp.zeros((SUB, LANES), jnp.float32)
    for buffer in (ping, pong):
        for c in range(tiles_across):
            buffer[c, 0:SUB, :] = zero
            buffer[c, SUB + rows : 2 * SUB + rows, :] = zero

    lane = lax.broadcasted_iota(jnp.int32, (SUB, LANES), 1)
    first, last = lane == 0, lane == LANES - 1

    def one_pass(source, store, after=None):
        for half in range(0, steps, SUB):
            center, right_moved, left_moved = {}, {}, {}

            def prepare(c):
                for i in range(half, half + SUB):
                    value = source[c, SUB + i * SUB : 2 * SUB + i * SUB, :]
                    center[c, i] = value
                    right_moved[c, i] = pltpu.roll(value, 1, 1)
                    left_moved[c, i] = pltpu.roll(value, LANES - 1, 1)

            prepare(0)
            for c in range(tiles_across):
                if c + 1 < tiles_across:
                    prepare(c + 1)
                for i in range(half, half + SUB):
                    at = slice(i * SUB, i * SUB + SUB)
                    up = source[c, SUB - 1 + i * SUB : 2 * SUB - 1 + i * SUB, :]
                    down = source[c, SUB + 1 + i * SUB : 2 * SUB + 1 + i * SUB, :]
                    left = jnp.where(first, right_moved[c - 1, i] if c > 0 else zero, right_moved[c, i])
                    right = jnp.where(last, left_moved[c + 1, i] if c + 1 < tiles_across else zero, left_moved[c, i])
                    around = (up + down) + (left + right)
                    store(i, c, own[c, at, :] * center[c, i] + lat[c, at, :] * around)
            if after:
                after(half // SUB)

    def into(buffer):
        def store(i, c, value):
            buffer[c, SUB + i * SUB : 2 * SUB + i * SUB, :] = value

        return store

    @pl.loop(0, count)
    def _(f):
        slot = f % 2
        load(f).wait()

        @pl.when(f + 2 < count)
        def _():
            load(f + 2).start()

        for c in range(tiles_across):
            ping[c, SUB : SUB + rows, :] = loaded[f, :, c * LANES : (c + 1) * LANES] * gain[c]
        one_pass(ping, into(pong))
        one_pass(pong, into(ping))

        @pl.when(f >= 2)
        def _():
            for half in range(2):
                deliver(slot, f - 2, half).wait()

        def finish(i, c, value):
            tile, part = i * SUB // tile_rows, i * SUB % tile_rows
            ready[slot, tile * tiles_across + c, part : part + SUB, :] = value

        one_pass(ping, finish, lambda half: deliver(slot, f, half).start())

    for f in range(count - 2, count):
        for half in range(2):
            deliver(f % 2, f, half).wait()


def smooth(core, table, frames, mine, other, tiles_down, tile_rows, chips):
    count, height, width = frames.shape
    across = 2 * chips
    devices = tiles_down * across
    return pl.pallas_call(
        functools.partial(smooth_body, tiles_down, tile_rows, chips),
        out_shape=jax.ShapeDtypeStruct((devices, count * tile_rows, LANES), jnp.float32),
        in_specs=[pl.BlockSpec(memory_space=pltpu.SMEM)] * 2
        + [pl.BlockSpec(memory_space=pltpu.HBM)]
        + [pl.BlockSpec(memory_space=pltpu.VMEM)] * 2,
        out_specs=pl.BlockSpec(memory_space=pltpu.HBM),
        scratch_shapes=[pltpu.VMEM((count, height, width), jnp.float32)]
        + [pltpu.VMEM((across, height, LANES), jnp.float32)] * 3
        + [pltpu.VMEM((across, height + 2 * SUB, LANES), jnp.float32)] * 2
        + [pltpu.VMEM((2, devices, tile_rows, LANES), jnp.float32)]
        + [pltpu.SemaphoreType.DMA((count,)), pltpu.SemaphoreType.DMA((2, 2))],
        compiler_params=pltpu.CompilerParams(vmem_limit_bytes=50 << 20),
        name="smooth",
    )(core, table, frames, mine, other)


def convolve_body(count, rows, x_ref, high_ref, low_ref, out_ref, loaded, high, low, ready, load_sem, early_sem, late_sem):
    quarters, chunk, _ = loaded.shape
    sources = chunk // (count * rows)
    outputs = out_ref.shape[2]
    half = outputs // 2
    first, second = slice(0, half), slice(half, outputs)
    groups = rows // ROW_GROUP

    def load(q):
        return pltpu.make_async_copy(x_ref.at[pl.ds(q * chunk, chunk)], loaded.at[q], load_sem.at[q])

    def save(k, columns, sem):
        part = slice(k * ROW_GROUP, (k + 1) * ROW_GROUP)
        return pltpu.make_async_copy(ready.at[part, :, columns], out_ref.at[part, :, columns], sem.at[k])

    def prepare(q, k):
        flat = loaded.at[q]
        for r in range(k * ROW_GROUP, (k + 1) * ROW_GROUP):
            parts = [flat[pl.ds(f * rows + r, sources, stride=count * rows), :] for f in range(count)]
            x = jnp.concatenate(parts, axis=0).T
            top = x.astype(jnp.bfloat16)
            at = (slice(r * LANES, (r + 1) * LANES), slice(q * LANES, (q + 1) * LANES))
            high[at] = top
            low[at] = (x - top.astype(jnp.float32)).astype(jnp.bfloat16)

    def product(k, terms, columns):
        at = (slice(k * ROW_GROUP * LANES, (k + 1) * ROW_GROUP * LANES), terms)

        def dot(a_ref, b_ref):
            return jnp.dot(a_ref[at], b_ref[terms, columns], preferred_element_type=jnp.float32)

        result = dot(high, high_ref) + (dot(high, low_ref) + dot(low, high_ref))
        return result.reshape(ROW_GROUP, LANES, half)

    for q in range(quarters):
        load(q).start()
    load(0).wait()
    for k in range(groups):
        prepare(0, k)
    load(1).wait()
    for k in range(groups):
        part = slice(k * ROW_GROUP, (k + 1) * ROW_GROUP)
        prepare(1, k)
        ready[part, :, first] = product(k, first, first)
        save(k, first, early_sem).start()
        ready[part, :, second] = product(k, first, second)
    load(2).wait()
    load(3).wait()
    for k in range(groups):
        part = slice(k * ROW_GROUP, (k + 1) * ROW_GROUP)
        prepare(2, k)
        prepare(3, k)
        ready[part, :, second] = ready[part, :, second] + product(k, second, second)
        save(k, second, late_sem).start()
    for k in range(groups):
        save(k, first, early_sem).wait()
        save(k, second, late_sem).wait()


def convolve(blocks, high, low, count, tile_rows):
    devices = blocks.shape[0]
    frames = high.shape[1]
    quarters = 4
    return pl.pallas_call(
        functools.partial(convolve_body, count, tile_rows),
        out_shape=jax.ShapeDtypeStruct((tile_rows, LANES, frames), jnp.float32),
        in_specs=[pl.BlockSpec(memory_space=pltpu.HBM)] + [pl.BlockSpec(memory_space=pltpu.VMEM)] * 2,
        out_specs=pl.BlockSpec(memory_space=pltpu.HBM),
        scratch_shapes=[pltpu.VMEM((quarters, devices // quarters * count * tile_rows, LANES), jnp.float32)]
        + [pltpu.VMEM((tile_rows * LANES, frames), jnp.bfloat16)] * 2
        + [pltpu.VMEM((tile_rows, LANES, frames), jnp.float32)]
        + [pltpu.SemaphoreType.DMA((quarters,))]
        + [pltpu.SemaphoreType.DMA((tile_rows // ROW_GROUP,))] * 2,
        compiler_params=pltpu.CompilerParams(vmem_limit_bytes=50 << 20),
        name="convolve",
    )(blocks.reshape(devices * count * tile_rows, LANES), high, low)


def lookup(classes, mask, entry, count):
    result = jnp.zeros(classes.shape, jnp.float32)
    for k in range(count):
        result = jnp.where(classes == k, entry(k), result)
    return jnp.where(mask != 0, result, 0.0)


def lateral_body(class_ref, mask_ref, effusivity_ref, conductivity_ref, map_ref, table_ref, shared_ref):
    count = conductivity_ref.shape[0]
    rates = [lateral_rate * conductivity_ref[k] for k in range(count)]
    shared = jnp.int32(0)
    for k in range(count):
        table_ref[0, k] = rates[k]
        table_ref[1, k] = flux_factor * effusivity_ref[k]
        for other in range(k):
            shared = shared | (rates[k] == rates[other]).astype(jnp.int32)
    shared_ref[0] = shared
    lateral = lookup(class_ref[...], mask_ref[...], lambda k: rates[k], count)
    for peer in range(map_ref.shape[0]):
        map_ref[peer] = lateral


def lateral_for(peers, class_index, surface_mask, effusivity, conductivity):
    smem, vmem = pl.BlockSpec(memory_space=pltpu.SMEM), pl.BlockSpec(memory_space=pltpu.VMEM)
    return pl.pallas_call(
        lateral_body,
        out_shape=(
            jax.ShapeDtypeStruct((peers, *class_index.shape), jnp.float32),
            jax.ShapeDtypeStruct((2, conductivity.shape[0]), jnp.float32),
            jax.ShapeDtypeStruct((1,), jnp.int32),
        ),
        in_specs=[vmem, vmem, smem, smem],
        out_specs=(vmem, smem, smem),
        name="lateral",
    )(class_index, surface_mask, effusivity, conductivity)


def per_device(frames, class_index, surface_mask, effusivity, conductivity):
    tiles_down, chips = lax.axis_size("row"), lax.axis_size("chip")
    tile_rows = class_index.shape[0]
    count = frames.shape[0]
    devices = tiles_down * chips * 2
    core = lax.axis_index("core")

    peers = tiles_down * chips
    lateral, table, shared = lateral_for(peers, class_index, surface_mask, effusivity, conductivity)

    def smoothed(maps):
        mine = lax.all_to_all(maps, ("row", "chip"), split_axis=0, concat_axis=0, tiled=True)
        other = lax.ppermute(mine, "core", [(0, 1), (1, 0)])
        return smooth(core[None].astype(jnp.int32), table, frames, mine, other, tiles_down, tile_rows, chips)

    def from_both():
        gain = lookup(class_index, surface_mask, lambda k: table[1, k], table.shape[1])
        return smoothed(jnp.concatenate([lateral, jnp.broadcast_to(gain[None], lateral.shape)], axis=1))

    blocks = lax.cond(shared[0] != 0, from_both, lambda: smoothed(lateral))

    frame_ids = jnp.arange(devices * count, dtype=jnp.int32)
    quarter = devices // 4
    source = frame_ids // (quarter * count) * quarter + frame_ids % quarter
    arrival = source * count + frame_ids // quarter % count
    kernel = kernel_from(frame_ids, arrival).T
    rounded = lax.reduce_precision(kernel, 8, 7)
    high, low = rounded.astype(jnp.bfloat16), (kernel - rounded).astype(jnp.bfloat16)

    received = lax.all_to_all(blocks, ALL, split_axis=0, concat_axis=0, tiled=True)
    return convolve(received, high, low, count, tile_rows)


def solution(mesh):
    cores = Mesh(mesh.devices.reshape(mesh.shape["row"], mesh.shape["col"] // 2, 2), ALL)
    tile = P("row", ("chip", "core"))
    in_specs = (P(ALL, None, None), tile, tile, P(), P())
    return jax.shard_map(
        per_device, mesh=cores, in_specs=in_specs, out_specs=P("row", ("chip", "core"), None), check_vma=False
    )
```

```python
import functools

import jax
import jax.numpy as jnp
from jax import lax
from jax.experimental import pallas as pl
from jax.experimental.pallas import tpu as pltpu
from jax.sharding import Mesh
from jax.sharding import PartitionSpec as P

LANES = 128
SUB = 8
ROW_GROUP = 2

flux_factor = 1.1283791670955126
lateral_rate = 0.24

ALL = ("row", "chip", "core")


def weights(lagged):
    clipped = jnp.maximum(lagged, 0.0)
    return jnp.where(lagged >= 0.0, 1.0 / (jnp.sqrt(clipped) + jnp.sqrt(clipped + 1.0)), 0.0)


def kernel_from(later, earlier):
    lagged = (later[:, None] - earlier[None, :]).astype(jnp.float32)
    return weights(lagged) - weights(lagged - 1.0)


def gain_of(maps, tile_rows, table_ref):
    if maps.shape[0] == 2 * tile_rows:
        return maps[tile_rows:]
    found = jnp.zeros_like(maps)
    for k in range(table_ref.shape[1]):
        found = jnp.where(maps == table_ref[0, k], table_ref[1, k], found)
    return found


def prime_body(tile_rows, table_ref, frames_ref, mine_ref, frame_ref, gain_ref, sem):
    load = pltpu.make_async_copy(frames_ref.at[0], frame_ref, sem)
    load.start()
    for part in range(mine_ref.shape[0]):
        gain_ref[part] = gain_of(mine_ref[part], tile_rows, table_ref)
    load.wait()


def prime(table, frames, mine, tile_rows):
    smem, vmem = pl.BlockSpec(memory_space=pltpu.SMEM), pl.BlockSpec(memory_space=pltpu.VMEM)
    return pl.pallas_call(
        functools.partial(prime_body, tile_rows),
        out_shape=(
            jax.ShapeDtypeStruct(frames.shape[1:], jnp.float32),
            jax.ShapeDtypeStruct((mine.shape[0], tile_rows, LANES), jnp.float32),
        ),
        in_specs=[smem, pl.BlockSpec(memory_space=pltpu.HBM), vmem],
        out_specs=(vmem, vmem),
        scratch_shapes=[pltpu.SemaphoreType.DMA],
        compiler_params=pltpu.CompilerParams(vmem_limit_bytes=50 << 20),
        cost_estimate=pl.CostEstimate(flops=16 << 18, bytes_accessed=4 << 20, transcendentals=0),
        name="prime",
    )(table, frames, mine)


def smooth_body(
    tiles_down, tile_rows, chips,
    core_ref, table_ref, frames_ref, frame_ref, gain_ref, mine_ref, other_ref, out_ref,
    loaded, gain, lat, own, ping, pong, ready, load_sem, store_sem,
):
    tiles_across = 2 * chips
    count, rows, _ = frames_ref.shape
    core = core_ref[0]
    steps = rows // SUB

    def load(f):
        return pltpu.make_async_copy(frames_ref.at[f], loaded.at[f - 1], load_sem.at[f - 1])

    def deliver(slot, f, half):
        part = pl.ds(pl.multiple_of(f * tile_rows, tile_rows), tile_rows)
        to = pl.ds(half * (tiles_down // 2) * tiles_across, tiles_down // 2 * tiles_across)
        return pltpu.make_async_copy(ready.at[slot, to], out_ref.at[to, part, :], store_sem.at[slot, half])

    load(1).start()
    for tile in range(tiles_down):
        for chip in range(chips):
            part = tile * chips + chip
            at = pl.ds(tile * tile_rows, tile_rows)
            maps = other_ref[part]
            gains = (gain_ref[part], gain_of(maps, tile_rows, table_ref))
            for index, lateral, factor in zip(
                (2 * chip + core, 2 * chip + 1 - core), (mine_ref[part, 0:tile_rows, :], maps[0:tile_rows]), gains
            ):
                gain[index, at, :] = factor
                lat[index, at, :] = lateral
                own[index, at, :] = 1.0 - 4.0 * lateral
    zero = jnp.zeros((SUB, LANES), jnp.float32)
    for buffer in (ping, pong):
        for c in range(tiles_across):
            buffer[c, 0:SUB, :] = zero
            buffer[c, SUB + rows : 2 * SUB + rows, :] = zero

    lane = lax.broadcasted_iota(jnp.int32, (SUB, LANES), 1)
    first, last = lane == 0, lane == LANES - 1

    def one_pass(source, store, after=None):
        for half in range(0, steps, SUB):
            center, right_moved, left_moved = {}, {}, {}

            def prepare(c):
                for i in range(half, half + SUB):
                    value = source[c, SUB + i * SUB : 2 * SUB + i * SUB, :]
                    center[c, i] = value
                    right_moved[c, i] = pltpu.roll(value, 1, 1)
                    left_moved[c, i] = pltpu.roll(value, LANES - 1, 1)

            prepare(0)
            for c in range(tiles_across):
                if c + 1 < tiles_across:
                    prepare(c + 1)
                for i in range(half, half + SUB):
                    at = slice(i * SUB, i * SUB + SUB)
                    up = source[c, SUB - 1 + i * SUB : 2 * SUB - 1 + i * SUB, :]
                    down = source[c, SUB + 1 + i * SUB : 2 * SUB + 1 + i * SUB, :]
                    left = jnp.where(first, right_moved[c - 1, i] if c > 0 else zero, right_moved[c, i])
                    right = jnp.where(last, left_moved[c + 1, i] if c + 1 < tiles_across else zero, left_moved[c, i])
                    around = (up + down) + (left + right)
                    store(i, c, own[c, at, :] * center[c, i] + lat[c, at, :] * around)
            if after:
                after(half // SUB)

    def into(buffer):
        def store(i, c, value):
            buffer[c, SUB + i * SUB : 2 * SUB + i * SUB, :] = value

        return store

    def enter(frame):
        for c in range(tiles_across):
            ping[c, SUB : SUB + rows, :] = frame[:, c * LANES : (c + 1) * LANES] * gain[c]

    enter(frame_ref)

    @pl.loop(0, count)
    def _(f):
        slot = f % 2

        @pl.when(f > 0)
        def _():
            load(f).wait()
            enter(loaded.at[f - 1])

        @pl.when(f + 1 < count)
        def _():
            @pl.when(f > 0)
            def _():
                load(f + 1).start()

        one_pass(ping, into(pong))
        one_pass(pong, into(ping))

        @pl.when(f >= 2)
        def _():
            for half in range(2):
                deliver(slot, f - 2, half).wait()

        def finish(i, c, value):
            tile, part = i * SUB // tile_rows, i * SUB % tile_rows
            ready[slot, tile * tiles_across + c, part : part + SUB, :] = value

        one_pass(ping, finish, lambda half: deliver(slot, f, half).start())

    for f in range(count - 2, count):
        for half in range(2):
            deliver(f % 2, f, half).wait()


def smooth(core, table, frames, frame, gain, mine, other, tiles_down, tile_rows, chips):
    count, height, width = frames.shape
    across = 2 * chips
    devices = tiles_down * across
    return pl.pallas_call(
        functools.partial(smooth_body, tiles_down, tile_rows, chips),
        out_shape=jax.ShapeDtypeStruct((devices, count * tile_rows, LANES), jnp.float32),
        in_specs=[pl.BlockSpec(memory_space=pltpu.SMEM)] * 2
        + [pl.BlockSpec(memory_space=pltpu.HBM)]
        + [pl.BlockSpec(memory_space=pltpu.VMEM)] * 4,
        out_specs=pl.BlockSpec(memory_space=pltpu.HBM),
        scratch_shapes=[pltpu.VMEM((count - 1, height, width), jnp.float32)]
        + [pltpu.VMEM((across, height, LANES), jnp.float32)] * 3
        + [pltpu.VMEM((across, height + 2 * SUB, LANES), jnp.float32)] * 2
        + [pltpu.VMEM((2, devices, tile_rows, LANES), jnp.float32)]
        + [pltpu.SemaphoreType.DMA((count - 1,)), pltpu.SemaphoreType.DMA((2, 2))],
        compiler_params=pltpu.CompilerParams(vmem_limit_bytes=50 << 20),
        name="smooth",
    )(core, table, frames, frame, gain, mine, other)


def convolve_body(count, rows, x_ref, high_ref, low_ref, out_ref, loaded, high, low, ready, load_sem, early_sem, late_sem):
    quarters, chunk, _ = loaded.shape
    sources = chunk // (count * rows)
    outputs = out_ref.shape[2]
    half = outputs // 2
    first, second = slice(0, half), slice(half, outputs)
    groups = rows // ROW_GROUP

    def load(q):
        return pltpu.make_async_copy(x_ref.at[pl.ds(q * chunk, chunk)], loaded.at[q], load_sem.at[q])

    def save(k, columns, sem):
        part = slice(k * ROW_GROUP, (k + 1) * ROW_GROUP)
        return pltpu.make_async_copy(ready.at[part, :, columns], out_ref.at[part, :, columns], sem.at[k])

    def prepare(q, k):
        flat = loaded.at[q]
        for r in range(k * ROW_GROUP, (k + 1) * ROW_GROUP):
            parts = [flat[pl.ds(f * rows + r, sources, stride=count * rows), :] for f in range(count)]
            x = jnp.concatenate(parts, axis=0).T
            top = x.astype(jnp.bfloat16)
            at = (slice(r * LANES, (r + 1) * LANES), slice(q * LANES, (q + 1) * LANES))
            high[at] = top
            low[at] = (x - top.astype(jnp.float32)).astype(jnp.bfloat16)

    def product(k, terms, columns):
        at = (slice(k * ROW_GROUP * LANES, (k + 1) * ROW_GROUP * LANES), terms)

        def dot(a_ref, b_ref):
            return jnp.dot(a_ref[at], b_ref[terms, columns], preferred_element_type=jnp.float32)

        result = dot(high, high_ref) + (dot(high, low_ref) + dot(low, high_ref))
        return result.reshape(ROW_GROUP, LANES, half)

    for q in range(quarters):
        load(q).start()
    load(0).wait()
    for k in range(groups):
        prepare(0, k)
    load(1).wait()
    prepare(1, 0)
    for k in range(groups):
        if k + 1 < groups:
            prepare(1, k + 1)
        else:
            load(2).wait()
            load(3).wait()
            prepare(2, 0)
            prepare(3, 0)
        ready[k * ROW_GROUP : (k + 1) * ROW_GROUP, :, first] = product(k, first, first)
        save(k, first, early_sem).start()
    for k in range(groups):
        if k + 1 < groups:
            prepare(2, k + 1)
            prepare(3, k + 1)
        ready[k * ROW_GROUP : (k + 1) * ROW_GROUP, :, second] = product(k, slice(0, outputs), second)
        save(k, second, late_sem).start()
    for k in range(groups):
        save(k, first, early_sem).wait()
        save(k, second, late_sem).wait()


def convolve(blocks, high, low, count, tile_rows):
    devices = blocks.shape[0]
    frames = high.shape[1]
    quarters = 4
    return pl.pallas_call(
        functools.partial(convolve_body, count, tile_rows),
        out_shape=jax.ShapeDtypeStruct((tile_rows, LANES, frames), jnp.float32),
        in_specs=[pl.BlockSpec(memory_space=pltpu.HBM)] + [pl.BlockSpec(memory_space=pltpu.VMEM)] * 2,
        out_specs=pl.BlockSpec(memory_space=pltpu.HBM),
        scratch_shapes=[pltpu.VMEM((quarters, devices // quarters * count * tile_rows, LANES), jnp.float32)]
        + [pltpu.VMEM((tile_rows * LANES, frames), jnp.bfloat16)] * 2
        + [pltpu.VMEM((tile_rows, LANES, frames), jnp.float32)]
        + [pltpu.SemaphoreType.DMA((quarters,))]
        + [pltpu.SemaphoreType.DMA((tile_rows // ROW_GROUP,))] * 2,
        compiler_params=pltpu.CompilerParams(vmem_limit_bytes=50 << 20),
        name="convolve",
    )(blocks.reshape(devices * count * tile_rows, LANES), high, low)


def lookup(classes, mask, entry, count):
    result = jnp.zeros(classes.shape, jnp.float32)
    for k in range(count):
        result = jnp.where(classes == k, entry(k), result)
    return jnp.where(mask != 0, result, 0.0)


def lateral_body(class_ref, mask_ref, effusivity_ref, conductivity_ref, map_ref, table_ref, shared_ref):
    count = conductivity_ref.shape[0]
    rates = [lateral_rate * conductivity_ref[k] for k in range(count)]
    shared = jnp.int32(0)
    for k in range(count):
        table_ref[0, k] = rates[k]
        table_ref[1, k] = flux_factor * effusivity_ref[k]
        for other in range(k):
            shared = shared | (rates[k] == rates[other]).astype(jnp.int32)
    shared_ref[0] = shared
    lateral = lookup(class_ref[...], mask_ref[...], lambda k: rates[k], count)
    for peer in range(map_ref.shape[0]):
        map_ref[peer] = lateral


def lateral_for(peers, class_index, surface_mask, effusivity, conductivity):
    smem, vmem = pl.BlockSpec(memory_space=pltpu.SMEM), pl.BlockSpec(memory_space=pltpu.VMEM)
    return pl.pallas_call(
        lateral_body,
        out_shape=(
            jax.ShapeDtypeStruct((peers, *class_index.shape), jnp.float32),
            jax.ShapeDtypeStruct((2, conductivity.shape[0]), jnp.float32),
            jax.ShapeDtypeStruct((1,), jnp.int32),
        ),
        in_specs=[vmem, vmem, smem, smem],
        out_specs=(vmem, smem, smem),
        name="lateral",
    )(class_index, surface_mask, effusivity, conductivity)


def per_device(frames, class_index, surface_mask, effusivity, conductivity):
    tiles_down, chips = lax.axis_size("row"), lax.axis_size("chip")
    tile_rows = class_index.shape[0]
    count = frames.shape[0]
    devices = tiles_down * chips * 2
    core = lax.axis_index("core")

    peers = tiles_down * chips
    lateral, table, shared = lateral_for(peers, class_index, surface_mask, effusivity, conductivity)

    def smoothed(maps):
        mine = lax.all_to_all(maps, ("row", "chip"), split_axis=0, concat_axis=0, tiled=True)
        other = lax.ppermute(mine, "core", [(0, 1), (1, 0)])
        frame, gain = prime(table, frames, mine, tile_rows)
        number = core[None].astype(jnp.int32)
        return smooth(number, table, frames, frame, gain, mine, other, tiles_down, tile_rows, chips)

    def from_both():
        gain = lookup(class_index, surface_mask, lambda k: table[1, k], table.shape[1])
        return smoothed(jnp.concatenate([lateral, jnp.broadcast_to(gain[None], lateral.shape)], axis=1))

    blocks = lax.cond(shared[0] != 0, from_both, lambda: smoothed(lateral))

    frame_ids = jnp.arange(devices * count, dtype=jnp.int32)
    quarter = devices // 4
    source = frame_ids // (quarter * count) * quarter + frame_ids % quarter
    arrival = source * count + frame_ids // quarter % count
    kernel = kernel_from(frame_ids, arrival).T
    rounded = lax.reduce_precision(kernel, 8, 7)
    high, low = rounded.astype(jnp.bfloat16), (kernel - rounded).astype(jnp.bfloat16)

    received = lax.all_to_all(blocks, ALL, split_axis=0, concat_axis=0, tiled=True)
    return convolve(received, high, low, count, tile_rows)


def solution(mesh):
    cores = Mesh(mesh.devices.reshape(mesh.shape["row"], mesh.shape["col"] // 2, 2), ALL)
    tile = P("row", ("chip", "core"))
    in_specs = (P(ALL, None, None), tile, tile, P(), P())
    return jax.shard_map(
        per_device, mesh=cores, in_specs=in_specs, out_specs=P("row", ("chip", "core"), None), check_vma=False
    )
```

```python
import functools

import jax
import jax.numpy as jnp
from jax import lax
from jax.experimental import pallas as pl
from jax.experimental.pallas import tpu as pltpu
from jax.sharding import Mesh
from jax.sharding import PartitionSpec as P

LANES = 128
SUB = 8
ROW_GROUP = 2

flux_factor = 1.1283791670955126
lateral_rate = 0.24

ALL = ("row", "chip", "core")


def weights(lagged):
    clipped = jnp.maximum(lagged, 0.0)
    return jnp.where(lagged >= 0.0, 1.0 / (jnp.sqrt(clipped) + jnp.sqrt(clipped + 1.0)), 0.0)


def kernel_from(later, earlier):
    lagged = (later[:, None] - earlier[None, :]).astype(jnp.float32)
    return weights(lagged) - weights(lagged - 1.0)


def gain_of(maps, tile_rows, table_ref):
    if maps.shape[0] == 2 * tile_rows:
        return maps[tile_rows:]
    found = jnp.zeros_like(maps)
    for k in range(table_ref.shape[1]):
        found = jnp.where(maps == table_ref[0, k], table_ref[1, k], found)
    return found


def prime_body(tile_rows, table_ref, frames_ref, mine_ref, frame_ref, gain_ref, sem):
    load = pltpu.make_async_copy(frames_ref.at[0], frame_ref, sem)
    load.start()
    for part in range(mine_ref.shape[0]):
        gain_ref[part] = gain_of(mine_ref[part], tile_rows, table_ref)
    load.wait()


def prime(table, frames, mine, tile_rows):
    smem, vmem = pl.BlockSpec(memory_space=pltpu.SMEM), pl.BlockSpec(memory_space=pltpu.VMEM)
    return pl.pallas_call(
        functools.partial(prime_body, tile_rows),
        out_shape=(
            jax.ShapeDtypeStruct(frames.shape[1:], jnp.float32),
            jax.ShapeDtypeStruct((mine.shape[0], tile_rows, LANES), jnp.float32),
        ),
        in_specs=[smem, pl.BlockSpec(memory_space=pltpu.HBM), vmem],
        out_specs=(vmem, vmem),
        scratch_shapes=[pltpu.SemaphoreType.DMA],
        compiler_params=pltpu.CompilerParams(vmem_limit_bytes=50 << 20),
        cost_estimate=pl.CostEstimate(flops=16 << 18, bytes_accessed=4 << 20, transcendentals=0),
        name="prime",
    )(table, frames, mine)


def smooth_body(
    tiles_down, tile_rows, chips,
    core_ref, table_ref, frames_ref, frame_ref, gain_ref, mine_ref, other_ref, out_ref,
    loaded, gain, lat, own, ping, pong, ready, load_sem, store_sem,
):
    tiles_across = 2 * chips
    count, rows, _ = frames_ref.shape
    core = core_ref[0]
    steps = rows // SUB

    def load(f):
        return pltpu.make_async_copy(frames_ref.at[f], loaded.at[f - 1], load_sem.at[f - 1])

    def deliver(slot, f, half):
        part = pl.ds(pl.multiple_of(f * tile_rows, tile_rows), tile_rows)
        to = pl.ds(half * (tiles_down // 2) * tiles_across, tiles_down // 2 * tiles_across)
        return pltpu.make_async_copy(ready.at[slot, to], out_ref.at[to, part, :], store_sem.at[slot, half])

    load(1).start()
    for tile in range(tiles_down):
        for chip in range(chips):
            part = tile * chips + chip
            at = pl.ds(tile * tile_rows, tile_rows)
            maps = other_ref[part]
            gains = (gain_ref[part], gain_of(maps, tile_rows, table_ref))
            for index, lateral, factor in zip(
                (2 * chip + core, 2 * chip + 1 - core), (mine_ref[part, 0:tile_rows, :], maps[0:tile_rows]), gains
            ):
                gain[index, at, :] = factor
                lat[index, at, :] = lateral
                own[index, at, :] = 1.0 - 4.0 * lateral
    zero = jnp.zeros((SUB, LANES), jnp.float32)
    for buffer in (ping, pong):
        for c in range(tiles_across):
            buffer[c, 0:SUB, :] = zero
            buffer[c, SUB + rows : 2 * SUB + rows, :] = zero

    lane = lax.broadcasted_iota(jnp.int32, (SUB, LANES), 1)
    first, last = lane == 0, lane == LANES - 1

    def one_pass(source, store, after=None):
        for half in range(0, steps, SUB):
            center, right_moved, left_moved = {}, {}, {}

            def prepare(c):
                for i in range(half, half + SUB):
                    value = source[c, SUB + i * SUB : 2 * SUB + i * SUB, :]
                    center[c, i] = value
                    right_moved[c, i] = pltpu.roll(value, 1, 1)
                    left_moved[c, i] = pltpu.roll(value, LANES - 1, 1)

            prepare(0)
            for c in range(tiles_across):
                if c + 1 < tiles_across:
                    prepare(c + 1)
                for i in range(half, half + SUB):
                    at = slice(i * SUB, i * SUB + SUB)
                    up = source[c, SUB - 1 + i * SUB : 2 * SUB - 1 + i * SUB, :]
                    down = source[c, SUB + 1 + i * SUB : 2 * SUB + 1 + i * SUB, :]
                    left = jnp.where(first, right_moved[c - 1, i] if c > 0 else zero, right_moved[c, i])
                    right = jnp.where(last, left_moved[c + 1, i] if c + 1 < tiles_across else zero, left_moved[c, i])
                    around = (up + down) + (left + right)
                    store(i, c, own[c, at, :] * center[c, i] + lat[c, at, :] * around)
            if after:
                after(half // SUB)

    def into(buffer):
        def store(i, c, value):
            buffer[c, SUB + i * SUB : 2 * SUB + i * SUB, :] = value

        return store

    def enter(frame):
        for c in range(tiles_across):
            ping[c, SUB : SUB + rows, :] = frame[:, c * LANES : (c + 1) * LANES] * gain[c]

    enter(frame_ref)

    @pl.loop(0, count)
    def _(f):
        slot = f % 2

        @pl.when(f > 0)
        def _():
            load(f).wait()
            enter(loaded.at[f - 1])

        @pl.when(f + 1 < count)
        def _():
            @pl.when(f > 0)
            def _():
                load(f + 1).start()

        one_pass(ping, into(pong))
        one_pass(pong, into(ping))

        @pl.when(f >= 2)
        def _():
            for half in range(2):
                deliver(slot, f - 2, half).wait()

        def finish(i, c, value):
            tile, part = i * SUB // tile_rows, i * SUB % tile_rows
            ready[slot, tile * tiles_across + c, part : part + SUB, :] = value

        one_pass(ping, finish, lambda half: deliver(slot, f, half).start())

    for f in range(count - 2, count):
        for half in range(2):
            deliver(f % 2, f, half).wait()


def smooth(core, table, frames, frame, gain, mine, other, tiles_down, tile_rows, chips):
    count, height, width = frames.shape
    across = 2 * chips
    devices = tiles_down * across
    return pl.pallas_call(
        functools.partial(smooth_body, tiles_down, tile_rows, chips),
        out_shape=jax.ShapeDtypeStruct((devices, count * tile_rows, LANES), jnp.float32),
        in_specs=[pl.BlockSpec(memory_space=pltpu.SMEM)] * 2
        + [pl.BlockSpec(memory_space=pltpu.HBM)]
        + [pl.BlockSpec(memory_space=pltpu.VMEM)] * 4,
        out_specs=pl.BlockSpec(memory_space=pltpu.HBM),
        scratch_shapes=[pltpu.VMEM((count - 1, height, width), jnp.float32)]
        + [pltpu.VMEM((across, height, LANES), jnp.float32)] * 3
        + [pltpu.VMEM((across, height + 2 * SUB, LANES), jnp.float32)] * 2
        + [pltpu.VMEM((2, devices, tile_rows, LANES), jnp.float32)]
        + [pltpu.SemaphoreType.DMA((count - 1,)), pltpu.SemaphoreType.DMA((2, 2))],
        compiler_params=pltpu.CompilerParams(vmem_limit_bytes=50 << 20),
        name="smooth",
    )(core, table, frames, frame, gain, mine, other)


def convolve_body(count, rows, x_ref, high_ref, low_ref, out_ref, loaded, high, low, ready, load_sem, early_sem, late_sem):
    quarters, sources, pitch, _ = loaded.shape
    outputs = out_ref.shape[2]
    half = outputs // 2
    first, second = slice(0, half), slice(half, outputs)
    groups = rows // ROW_GROUP

    def load(q):
        part = pl.ds(q * sources, sources)
        return pltpu.make_async_copy(x_ref.at[part], loaded.at[q, :, 0 : count * rows, :], load_sem.at[q])

    def save(k, columns, sem):
        part = slice(k * ROW_GROUP, (k + 1) * ROW_GROUP)
        return pltpu.make_async_copy(ready.at[part, :, columns], out_ref.at[part, :, columns], sem.at[k])

    def prepare(q, k):
        flat = loaded.at[q].reshape(sources * pitch, LANES)
        for r in range(k * ROW_GROUP, (k + 1) * ROW_GROUP):
            parts = [flat[pl.ds(f * rows + r, sources, stride=pitch), :] for f in range(count)]
            x = jnp.concatenate(parts, axis=0).T
            top = x.astype(jnp.bfloat16)
            at = (slice(r * LANES, (r + 1) * LANES), slice(q * LANES, (q + 1) * LANES))
            high[at] = top
            low[at] = (x - top.astype(jnp.float32)).astype(jnp.bfloat16)

    def product(k, terms, columns):
        at = (slice(k * ROW_GROUP * LANES, (k + 1) * ROW_GROUP * LANES), terms)

        def dot(a_ref, b_ref):
            return jnp.dot(a_ref[at], b_ref[terms, columns], preferred_element_type=jnp.float32)

        result = dot(high, high_ref) + (dot(high, low_ref) + dot(low, high_ref))
        return result.reshape(ROW_GROUP, LANES, half)

    for q in range(quarters):
        load(q).start()
    load(0).wait()
    for k in range(groups):
        prepare(0, k)
    load(1).wait()
    prepare(1, 0)
    for k in range(groups):
        if k + 1 < groups:
            prepare(1, k + 1)
        else:
            load(2).wait()
            load(3).wait()
            prepare(2, 0)
            prepare(3, 0)
        ready[k * ROW_GROUP : (k + 1) * ROW_GROUP, :, first] = product(k, first, first)
        save(k, first, early_sem).start()
    for k in range(groups):
        if k + 1 < groups:
            prepare(2, k + 1)
            prepare(3, k + 1)
        ready[k * ROW_GROUP : (k + 1) * ROW_GROUP, :, second] = product(k, slice(0, outputs), second)
        save(k, second, late_sem).start()
    for k in range(groups):
        save(k, first, early_sem).wait()
        save(k, second, late_sem).wait()


def convolve(blocks, high, low, count, tile_rows):
    devices = blocks.shape[0]
    frames = high.shape[1]
    quarters = 4
    return pl.pallas_call(
        functools.partial(convolve_body, count, tile_rows),
        out_shape=jax.ShapeDtypeStruct((tile_rows, LANES, frames), jnp.float32),
        in_specs=[pl.BlockSpec(memory_space=pltpu.HBM)] + [pl.BlockSpec(memory_space=pltpu.VMEM)] * 2,
        out_specs=pl.BlockSpec(memory_space=pltpu.HBM),
        scratch_shapes=[pltpu.VMEM((quarters, devices // quarters, count * tile_rows + SUB, LANES), jnp.float32)]
        + [pltpu.VMEM((tile_rows * LANES, frames), jnp.bfloat16)] * 2
        + [pltpu.VMEM((tile_rows, LANES, frames), jnp.float32)]
        + [pltpu.SemaphoreType.DMA((quarters,))]
        + [pltpu.SemaphoreType.DMA((tile_rows // ROW_GROUP,))] * 2,
        compiler_params=pltpu.CompilerParams(vmem_limit_bytes=50 << 20),
        name="convolve",
    )(blocks, high, low)


def lookup(classes, mask, entry, count):
    result = jnp.zeros(classes.shape, jnp.float32)
    for k in range(count):
        result = jnp.where(classes == k, entry(k), result)
    return jnp.where(mask != 0, result, 0.0)


def lateral_body(class_ref, mask_ref, effusivity_ref, conductivity_ref, map_ref, table_ref, shared_ref):
    count = conductivity_ref.shape[0]
    rates = [lateral_rate * conductivity_ref[k] for k in range(count)]
    shared = jnp.int32(0)
    for k in range(count):
        table_ref[0, k] = rates[k]
        table_ref[1, k] = flux_factor * effusivity_ref[k]
        for other in range(k):
            shared = shared | (rates[k] == rates[other]).astype(jnp.int32)
    shared_ref[0] = shared
    lateral = lookup(class_ref[...], mask_ref[...], lambda k: rates[k], count)
    for peer in range(map_ref.shape[0]):
        map_ref[peer] = lateral


def lateral_for(peers, class_index, surface_mask, effusivity, conductivity):
    smem, vmem = pl.BlockSpec(memory_space=pltpu.SMEM), pl.BlockSpec(memory_space=pltpu.VMEM)
    return pl.pallas_call(
        lateral_body,
        out_shape=(
            jax.ShapeDtypeStruct((peers, *class_index.shape), jnp.float32),
            jax.ShapeDtypeStruct((2, conductivity.shape[0]), jnp.float32),
            jax.ShapeDtypeStruct((1,), jnp.int32),
        ),
        in_specs=[vmem, vmem, smem, smem],
        out_specs=(vmem, smem, smem),
        name="lateral",
    )(class_index, surface_mask, effusivity, conductivity)


def per_device(frames, class_index, surface_mask, effusivity, conductivity):
    tiles_down, chips = lax.axis_size("row"), lax.axis_size("chip")
    tile_rows = class_index.shape[0]
    count = frames.shape[0]
    devices = tiles_down * chips * 2
    core = lax.axis_index("core")

    peers = tiles_down * chips
    lateral, table, shared = lateral_for(peers, class_index, surface_mask, effusivity, conductivity)

    def smoothed(maps):
        mine = lax.all_to_all(maps, ("row", "chip"), split_axis=0, concat_axis=0, tiled=True)
        other = lax.ppermute(mine, "core", [(0, 1), (1, 0)])
        frame, gain = prime(table, frames, mine, tile_rows)
        number = core[None].astype(jnp.int32)
        return smooth(number, table, frames, frame, gain, mine, other, tiles_down, tile_rows, chips)

    def from_both():
        gain = lookup(class_index, surface_mask, lambda k: table[1, k], table.shape[1])
        return smoothed(jnp.concatenate([lateral, jnp.broadcast_to(gain[None], lateral.shape)], axis=1))

    blocks = lax.cond(shared[0] != 0, from_both, lambda: smoothed(lateral))

    frame_ids = jnp.arange(devices * count, dtype=jnp.int32)
    quarter = devices // 4
    source = frame_ids // (quarter * count) * quarter + frame_ids % quarter
    arrival = source * count + frame_ids // quarter % count
    kernel = kernel_from(frame_ids, arrival).T
    rounded = lax.reduce_precision(kernel, 8, 7)
    high, low = rounded.astype(jnp.bfloat16), (kernel - rounded).astype(jnp.bfloat16)

    received = lax.all_to_all(blocks, ALL, split_axis=0, concat_axis=0, tiled=True)
    return convolve(received, high, low, count, tile_rows)


def solution(mesh):
    cores = Mesh(mesh.devices.reshape(mesh.shape["row"], mesh.shape["col"] // 2, 2), ALL)
    tile = P("row", ("chip", "core"))
    in_specs = (P(ALL, None, None), tile, tile, P(), P())
    return jax.shard_map(
        per_device, mesh=cores, in_specs=in_specs, out_specs=P("row", ("chip", "core"), None), check_vma=False
    )
```

```python
import functools

import jax
import jax.numpy as jnp
from jax import lax
from jax.experimental import pallas as pl
from jax.experimental.pallas import tpu as pltpu
from jax.sharding import Mesh
from jax.sharding import PartitionSpec as P

LANES = 128
SUB = 8
ROW_GROUP = 2
PRODUCT_EVERY = 4

flux_factor = 1.1283791670955126
lateral_rate = 0.24

ALL = ("row", "chip", "core")


def weights(lagged):
    clipped = jnp.maximum(lagged, 0.0)
    return jnp.where(lagged >= 0.0, 1.0 / (jnp.sqrt(clipped) + jnp.sqrt(clipped + 1.0)), 0.0)


def kernel_from(later, earlier):
    lagged = (later[:, None] - earlier[None, :]).astype(jnp.float32)
    return weights(lagged) - weights(lagged - 1.0)


def gain_of(maps, tile_rows, table_ref):
    if maps.shape[0] == 2 * tile_rows:
        return maps[tile_rows:]
    found = jnp.zeros_like(maps)
    for k in range(table_ref.shape[1]):
        found = jnp.where(maps == table_ref[0, k], table_ref[1, k], found)
    return found


def prime_body(tile_rows, table_ref, frames_ref, mine_ref, frame_ref, gain_ref, sem):
    load = pltpu.make_async_copy(frames_ref.at[0], frame_ref, sem)
    load.start()
    for part in range(mine_ref.shape[0]):
        gain_ref[part] = gain_of(mine_ref[part], tile_rows, table_ref)
    load.wait()


def prime(table, frames, mine, tile_rows):
    smem, vmem = pl.BlockSpec(memory_space=pltpu.SMEM), pl.BlockSpec(memory_space=pltpu.VMEM)
    return pl.pallas_call(
        functools.partial(prime_body, tile_rows),
        out_shape=(
            jax.ShapeDtypeStruct(frames.shape[1:], jnp.float32),
            jax.ShapeDtypeStruct((mine.shape[0], tile_rows, LANES), jnp.float32),
        ),
        in_specs=[smem, pl.BlockSpec(memory_space=pltpu.HBM), vmem],
        out_specs=(vmem, vmem),
        scratch_shapes=[pltpu.SemaphoreType.DMA],
        compiler_params=pltpu.CompilerParams(vmem_limit_bytes=50 << 20),
        cost_estimate=pl.CostEstimate(flops=16 << 18, bytes_accessed=4 << 20, transcendentals=0),
        name="prime",
    )(table, frames, mine)


def smooth_body(
    tiles_down, tile_rows, chips,
    core_ref, table_ref, frames_ref, frame_ref, gain_ref, mine_ref, other_ref, out_ref,
    loaded, gain, lat, own, ping, pong, ready, load_sem, store_sem,
):
    tiles_across = 2 * chips
    count, rows, _ = frames_ref.shape
    core = core_ref[0]
    steps = rows // SUB

    def load(f):
        return pltpu.make_async_copy(frames_ref.at[f], loaded.at[f - 1], load_sem.at[f - 1])

    def deliver(slot, f, half):
        part = pl.ds(pl.multiple_of(f * tile_rows, tile_rows), tile_rows)
        to = pl.ds(half * (tiles_down // 2) * tiles_across, tiles_down // 2 * tiles_across)
        return pltpu.make_async_copy(ready.at[slot, to], out_ref.at[to, part, :], store_sem.at[slot, half])

    load(1).start()
    for tile in range(tiles_down):
        for chip in range(chips):
            part = tile * chips + chip
            at = pl.ds(tile * tile_rows, tile_rows)
            maps = other_ref[part]
            gains = (gain_ref[part], gain_of(maps, tile_rows, table_ref))
            for index, lateral, factor in zip(
                (2 * chip + core, 2 * chip + 1 - core), (mine_ref[part, 0:tile_rows, :], maps[0:tile_rows]), gains
            ):
                gain[index, at, :] = factor
                lat[index, at, :] = lateral
                own[index, at, :] = 1.0 - 4.0 * lateral
    zero = jnp.zeros((SUB, LANES), jnp.float32)
    for buffer in (ping, pong):
        for c in range(tiles_across):
            buffer[c, 0:SUB, :] = zero
            buffer[c, SUB + rows : 2 * SUB + rows, :] = zero

    lane = lax.broadcasted_iota(jnp.int32, (SUB, LANES), 1)
    first, last = lane == 0, lane == LANES - 1
    source_lane = lax.broadcasted_iota(jnp.int32, (2 * LANES, 2 * LANES), 0) % LANES
    target_lane = lax.broadcasted_iota(jnp.int32, (2 * LANES, 2 * LANES), 1)
    wanted = jnp.where(target_lane < LANES, target_lane + LANES - 1, target_lane + 1) % LANES
    both_moves = (source_lane == wanted).astype(jnp.float32).astype(jnp.bfloat16)

    def one_pass(source, store, after=None):
        for half in range(0, steps, SUB):
            center, right_moved, left_moved = {}, {}, {}

            def prepare(c):
                by_product = c % PRODUCT_EVERY == 0
                if by_product:
                    block = source[c, SUB + half * SUB : SUB + (half + SUB) * SUB, :]
                    top = block.astype(jnp.bfloat16)
                    rest = (block - top.astype(jnp.float32)).astype(jnp.bfloat16)
                    terms = jnp.concatenate([top, rest], axis=1)
                    moved = jnp.dot(terms, both_moves, preferred_element_type=jnp.float32)
                for i in range(half, half + SUB):
                    value = source[c, SUB + i * SUB : 2 * SUB + i * SUB, :]
                    center[c, i] = value
                    if by_product:
                        at = slice((i - half) * SUB, (i - half + 1) * SUB)
                        right_moved[c, i], left_moved[c, i] = moved[at, :LANES], moved[at, LANES:]
                    else:
                        right_moved[c, i] = pltpu.roll(value, 1, 1)
                        left_moved[c, i] = pltpu.roll(value, LANES - 1, 1)

            prepare(0)
            for c in range(tiles_across):
                if c + 1 < tiles_across:
                    prepare(c + 1)
                for i in range(half, half + SUB):
                    at = slice(i * SUB, i * SUB + SUB)
                    up = source[c, SUB - 1 + i * SUB : 2 * SUB - 1 + i * SUB, :]
                    down = source[c, SUB + 1 + i * SUB : 2 * SUB + 1 + i * SUB, :]
                    left = jnp.where(first, right_moved[c - 1, i] if c > 0 else zero, right_moved[c, i])
                    right = jnp.where(last, left_moved[c + 1, i] if c + 1 < tiles_across else zero, left_moved[c, i])
                    around = (up + down) + (left + right)
                    store(i, c, own[c, at, :] * center[c, i] + lat[c, at, :] * around)
            if after:
                after(half // SUB)

    def into(buffer):
        def store(i, c, value):
            buffer[c, SUB + i * SUB : 2 * SUB + i * SUB, :] = value

        return store

    def enter(frame):
        for c in range(tiles_across):
            ping[c, SUB : SUB + rows, :] = frame[:, c * LANES : (c + 1) * LANES] * gain[c]

    enter(frame_ref)

    @pl.loop(0, count)
    def _(f):
        slot = f % 2

        @pl.when(f > 0)
        def _():
            load(f).wait()
            enter(loaded.at[f - 1])

        @pl.when(f + 1 < count)
        def _():
            @pl.when(f > 0)
            def _():
                load(f + 1).start()

        one_pass(ping, into(pong))
        one_pass(pong, into(ping))

        @pl.when(f >= 2)
        def _():
            for half in range(2):
                deliver(slot, f - 2, half).wait()

        def finish(i, c, value):
            tile, part = i * SUB // tile_rows, i * SUB % tile_rows
            ready[slot, tile * tiles_across + c, part : part + SUB, :] = value

        one_pass(ping, finish, lambda half: deliver(slot, f, half).start())

    for f in range(count - 2, count):
        for half in range(2):
            deliver(f % 2, f, half).wait()


def smooth(core, table, frames, frame, gain, mine, other, tiles_down, tile_rows, chips):
    count, height, width = frames.shape
    across = 2 * chips
    devices = tiles_down * across
    return pl.pallas_call(
        functools.partial(smooth_body, tiles_down, tile_rows, chips),
        out_shape=jax.ShapeDtypeStruct((devices, count * tile_rows, LANES), jnp.float32),
        in_specs=[pl.BlockSpec(memory_space=pltpu.SMEM)] * 2
        + [pl.BlockSpec(memory_space=pltpu.HBM)]
        + [pl.BlockSpec(memory_space=pltpu.VMEM)] * 4,
        out_specs=pl.BlockSpec(memory_space=pltpu.HBM),
        scratch_shapes=[pltpu.VMEM((count - 1, height, width), jnp.float32)]
        + [pltpu.VMEM((across, height, LANES), jnp.float32)] * 3
        + [pltpu.VMEM((across, height + 2 * SUB, LANES), jnp.float32)] * 2
        + [pltpu.VMEM((2, devices, tile_rows, LANES), jnp.float32)]
        + [pltpu.SemaphoreType.DMA((count - 1,)), pltpu.SemaphoreType.DMA((2, 2))],
        compiler_params=pltpu.CompilerParams(vmem_limit_bytes=50 << 20),
        name="smooth",
    )(core, table, frames, frame, gain, mine, other)


def convolve_body(count, rows, x_ref, high_ref, low_ref, out_ref, loaded, high, low, ready, load_sem, early_sem, late_sem):
    quarters, sources, pitch, _ = loaded.shape
    outputs = out_ref.shape[2]
    half = outputs // 2
    first, second = slice(0, half), slice(half, outputs)
    groups = rows // ROW_GROUP

    def load(q):
        part = pl.ds(q * sources, sources)
        return pltpu.make_async_copy(x_ref.at[part], loaded.at[q, :, 0 : count * rows, :], load_sem.at[q])

    def save(k, columns, sem):
        part = slice(k * ROW_GROUP, (k + 1) * ROW_GROUP)
        return pltpu.make_async_copy(ready.at[part, :, columns], out_ref.at[part, :, columns], sem.at[k])

    def prepare(q, k):
        flat = loaded.at[q].reshape(sources * pitch, LANES)
        for r in range(k * ROW_GROUP, (k + 1) * ROW_GROUP):
            parts = [flat[pl.ds(f * rows + r, sources, stride=pitch), :] for f in range(count)]
            x = jnp.concatenate(parts, axis=0).T
            top = x.astype(jnp.bfloat16)
            at = (slice(r * LANES, (r + 1) * LANES), slice(q * LANES, (q + 1) * LANES))
            high[at] = top
            low[at] = (x - top.astype(jnp.float32)).astype(jnp.bfloat16)

    def product(k, terms, columns):
        at = (slice(k * ROW_GROUP * LANES, (k + 1) * ROW_GROUP * LANES), terms)

        def dot(a_ref, b_ref):
            return jnp.dot(a_ref[at], b_ref[terms, columns], preferred_element_type=jnp.float32)

        result = dot(high, high_ref) + (dot(high, low_ref) + dot(low, high_ref))
        return result.reshape(ROW_GROUP, LANES, half)

    for q in range(quarters):
        load(q).start()
    load(0).wait()
    for k in range(groups):
        prepare(0, k)
    load(1).wait()
    prepare(1, 0)
    for k in range(groups):
        if k + 1 < groups:
            prepare(1, k + 1)
        else:
            load(2).wait()
            load(3).wait()
            prepare(2, 0)
            prepare(3, 0)
        ready[k * ROW_GROUP : (k + 1) * ROW_GROUP, :, first] = product(k, first, first)
        save(k, first, early_sem).start()
    for k in range(groups):
        if k + 1 < groups:
            prepare(2, k + 1)
            prepare(3, k + 1)
        ready[k * ROW_GROUP : (k + 1) * ROW_GROUP, :, second] = product(k, slice(0, outputs), second)
        save(k, second, late_sem).start()
    for k in range(groups):
        save(k, first, early_sem).wait()
        save(k, second, late_sem).wait()


def convolve(blocks, high, low, count, tile_rows):
    devices = blocks.shape[0]
    frames = high.shape[1]
    quarters = 4
    return pl.pallas_call(
        functools.partial(convolve_body, count, tile_rows),
        out_shape=jax.ShapeDtypeStruct((tile_rows, LANES, frames), jnp.float32),
        in_specs=[pl.BlockSpec(memory_space=pltpu.HBM)] + [pl.BlockSpec(memory_space=pltpu.VMEM)] * 2,
        out_specs=pl.BlockSpec(memory_space=pltpu.HBM),
        scratch_shapes=[pltpu.VMEM((quarters, devices // quarters, count * tile_rows + SUB, LANES), jnp.float32)]
        + [pltpu.VMEM((tile_rows * LANES, frames), jnp.bfloat16)] * 2
        + [pltpu.VMEM((tile_rows, LANES, frames), jnp.float32)]
        + [pltpu.SemaphoreType.DMA((quarters,))]
        + [pltpu.SemaphoreType.DMA((tile_rows // ROW_GROUP,))] * 2,
        compiler_params=pltpu.CompilerParams(vmem_limit_bytes=50 << 20),
        name="convolve",
    )(blocks, high, low)


def lookup(classes, mask, entry, count):
    result = jnp.zeros(classes.shape, jnp.float32)
    for k in range(count):
        result = jnp.where(classes == k, entry(k), result)
    return jnp.where(mask != 0, result, 0.0)


def lateral_body(class_ref, mask_ref, effusivity_ref, conductivity_ref, map_ref, table_ref, shared_ref):
    count = conductivity_ref.shape[0]
    rates = [lateral_rate * conductivity_ref[k] for k in range(count)]
    shared = jnp.int32(0)
    for k in range(count):
        table_ref[0, k] = rates[k]
        table_ref[1, k] = flux_factor * effusivity_ref[k]
        for other in range(k):
            shared = shared | (rates[k] == rates[other]).astype(jnp.int32)
    shared_ref[0] = shared
    lateral = lookup(class_ref[...], mask_ref[...], lambda k: rates[k], count)
    for peer in range(map_ref.shape[0]):
        map_ref[peer] = lateral


def lateral_for(peers, class_index, surface_mask, effusivity, conductivity):
    smem, vmem = pl.BlockSpec(memory_space=pltpu.SMEM), pl.BlockSpec(memory_space=pltpu.VMEM)
    return pl.pallas_call(
        lateral_body,
        out_shape=(
            jax.ShapeDtypeStruct((peers, *class_index.shape), jnp.float32),
            jax.ShapeDtypeStruct((2, conductivity.shape[0]), jnp.float32),
            jax.ShapeDtypeStruct((1,), jnp.int32),
        ),
        in_specs=[vmem, vmem, smem, smem],
        out_specs=(vmem, smem, smem),
        name="lateral",
    )(class_index, surface_mask, effusivity, conductivity)


def per_device(frames, class_index, surface_mask, effusivity, conductivity):
    tiles_down, chips = lax.axis_size("row"), lax.axis_size("chip")
    tile_rows = class_index.shape[0]
    count = frames.shape[0]
    devices = tiles_down * chips * 2
    core = lax.axis_index("core")

    peers = tiles_down * chips
    lateral, table, shared = lateral_for(peers, class_index, surface_mask, effusivity, conductivity)

    def smoothed(maps):
        mine = lax.all_to_all(maps, ("row", "chip"), split_axis=0, concat_axis=0, tiled=True)
        other = lax.ppermute(mine, "core", [(0, 1), (1, 0)])
        frame, gain = prime(table, frames, mine, tile_rows)
        number = core[None].astype(jnp.int32)
        return smooth(number, table, frames, frame, gain, mine, other, tiles_down, tile_rows, chips)

    def from_both():
        gain = lookup(class_index, surface_mask, lambda k: table[1, k], table.shape[1])
        return smoothed(jnp.concatenate([lateral, jnp.broadcast_to(gain[None], lateral.shape)], axis=1))

    blocks = lax.cond(shared[0] != 0, from_both, lambda: smoothed(lateral))

    frame_ids = jnp.arange(devices * count, dtype=jnp.int32)
    quarter = devices // 4
    source = frame_ids // (quarter * count) * quarter + frame_ids % quarter
    arrival = source * count + frame_ids // quarter % count
    kernel = kernel_from(frame_ids, arrival).T
    rounded = lax.reduce_precision(kernel, 8, 7)
    high, low = rounded.astype(jnp.bfloat16), (kernel - rounded).astype(jnp.bfloat16)

    received = lax.all_to_all(blocks, ALL, split_axis=0, concat_axis=0, tiled=True)
    return convolve(received, high, low, count, tile_rows)


def solution(mesh):
    cores = Mesh(mesh.devices.reshape(mesh.shape["row"], mesh.shape["col"] // 2, 2), ALL)
    tile = P("row", ("chip", "core"))
    in_specs = (P(ALL, None, None), tile, tile, P(), P())
    return jax.shard_map(
        per_device, mesh=cores, in_specs=in_specs, out_specs=P("row", ("chip", "core"), None), check_vma=False
    )
```

```python
import functools

import jax
import jax.numpy as jnp
from jax import lax
from jax.experimental import pallas as pl
from jax.experimental.pallas import tpu as pltpu
from jax.sharding import Mesh
from jax.sharding import PartitionSpec as P

LANES = 128
SUB = 8
ROW_GROUP = 2
PRODUCT_EVERY = 4

flux_factor = 1.1283791670955126
lateral_rate = 0.24

ALL = ("row", "chip", "core")


def weights(lagged):
    clipped = jnp.maximum(lagged, 0.0)
    return jnp.where(lagged >= 0.0, 1.0 / (jnp.sqrt(clipped) + jnp.sqrt(clipped + 1.0)), 0.0)


def kernel_from(later, earlier):
    lagged = (later[:, None] - earlier[None, :]).astype(jnp.float32)
    return weights(lagged) - weights(lagged - 1.0)


def gain_of(maps, tile_rows, table_ref):
    if maps.shape[0] == 2 * tile_rows:
        return maps[tile_rows:]
    found = jnp.zeros_like(maps)
    for k in range(table_ref.shape[1]):
        found = jnp.where(maps == table_ref[0, k], table_ref[1, k], found)
    return found


def prime_body(tile_rows, table_ref, frames_ref, mine_ref, frame_ref, gain_ref, sem):
    load = pltpu.make_async_copy(frames_ref.at[0], frame_ref, sem)
    load.start()
    for part in range(mine_ref.shape[0]):
        gain_ref[part] = gain_of(mine_ref[part], tile_rows, table_ref)
    load.wait()


def prime(table, frames, mine, tile_rows):
    smem, vmem = pl.BlockSpec(memory_space=pltpu.SMEM), pl.BlockSpec(memory_space=pltpu.VMEM)
    return pl.pallas_call(
        functools.partial(prime_body, tile_rows),
        out_shape=(
            jax.ShapeDtypeStruct(frames.shape[1:], jnp.float32),
            jax.ShapeDtypeStruct((mine.shape[0], tile_rows, LANES), jnp.float32),
        ),
        in_specs=[smem, pl.BlockSpec(memory_space=pltpu.HBM), vmem],
        out_specs=(vmem, vmem),
        scratch_shapes=[pltpu.SemaphoreType.DMA],
        compiler_params=pltpu.CompilerParams(vmem_limit_bytes=50 << 20),
        cost_estimate=pl.CostEstimate(flops=16 << 18, bytes_accessed=4 << 20, transcendentals=0),
        name="prime",
    )(table, frames, mine)


def smooth_body(
    tiles_down, tile_rows, chips,
    core_ref, table_ref, frames_ref, frame_ref, gain_ref, mine_ref, other_ref, out_ref,
    loaded, gain, lat, own, ping, pong, ready, load_sem, store_sem,
):
    tiles_across = 2 * chips
    count, rows, _ = frames_ref.shape
    core = core_ref[0]
    steps = rows // SUB

    def load(f):
        return pltpu.make_async_copy(frames_ref.at[f], loaded.at[f - 1], load_sem.at[f - 1])

    def deliver(slot, f, half):
        part = pl.ds(pl.multiple_of(f * tile_rows, tile_rows), tile_rows)
        to = pl.ds(half * (tiles_down // 2) * tiles_across, tiles_down // 2 * tiles_across)
        return pltpu.make_async_copy(ready.at[slot, to, 0:tile_rows, :], out_ref.at[to, part, :], store_sem.at[slot, half])

    load(1).start()
    for tile in range(tiles_down):
        for chip in range(chips):
            part = tile * chips + chip
            at = pl.ds(tile * tile_rows, tile_rows)
            maps = other_ref[part]
            gains = (gain_ref[part], gain_of(maps, tile_rows, table_ref))
            for index, lateral, factor in zip(
                (2 * chip + core, 2 * chip + 1 - core), (mine_ref[part, 0:tile_rows, :], maps[0:tile_rows]), gains
            ):
                gain[index, at, :] = factor
                lat[index, at, :] = lateral
                own[index, at, :] = 1.0 - 4.0 * lateral
    zero = jnp.zeros((SUB, LANES), jnp.float32)
    for buffer in (ping, pong):
        for c in range(tiles_across):
            buffer[c, 0:SUB, :] = zero
            buffer[c, SUB + rows : 2 * SUB + rows, :] = zero

    lane = lax.broadcasted_iota(jnp.int32, (SUB, LANES), 1)
    first, last = lane == 0, lane == LANES - 1
    source_lane = lax.broadcasted_iota(jnp.int32, (2 * LANES, 2 * LANES), 0) % LANES
    target_lane = lax.broadcasted_iota(jnp.int32, (2 * LANES, 2 * LANES), 1)
    wanted = jnp.where(target_lane < LANES, target_lane + LANES - 1, target_lane + 1) % LANES
    both_moves = (source_lane == wanted).astype(jnp.float32).astype(jnp.bfloat16)

    def one_pass(source, store, after=None):
        for half in range(0, steps, SUB):
            center, right_moved, left_moved = {}, {}, {}

            def prepare(c):
                by_product = c % PRODUCT_EVERY == 0
                if by_product:
                    block = source[c, SUB + half * SUB : SUB + (half + SUB) * SUB, :]
                    top = block.astype(jnp.bfloat16)
                    rest = (block - top.astype(jnp.float32)).astype(jnp.bfloat16)
                    terms = jnp.concatenate([top, rest], axis=1)
                    moved = jnp.dot(terms, both_moves, preferred_element_type=jnp.float32)
                for i in range(half, half + SUB):
                    value = source[c, SUB + i * SUB : 2 * SUB + i * SUB, :]
                    center[c, i] = value
                    if by_product:
                        at = slice((i - half) * SUB, (i - half + 1) * SUB)
                        right_moved[c, i], left_moved[c, i] = moved[at, :LANES], moved[at, LANES:]
                    else:
                        right_moved[c, i] = pltpu.roll(value, 1, 1)
                        left_moved[c, i] = pltpu.roll(value, LANES - 1, 1)

            prepare(0)
            prepare(1)
            for c in range(tiles_across):
                if c + 2 < tiles_across:
                    prepare(c + 2)
                for i in range(half, half + SUB):
                    at = slice(i * SUB, i * SUB + SUB)
                    up = source[c, SUB - 1 + i * SUB : 2 * SUB - 1 + i * SUB, :]
                    down = source[c, SUB + 1 + i * SUB : 2 * SUB + 1 + i * SUB, :]
                    left = jnp.where(first, right_moved[c - 1, i] if c > 0 else zero, right_moved[c, i])
                    right = jnp.where(last, left_moved[c + 1, i] if c + 1 < tiles_across else zero, left_moved[c, i])
                    around = (up + down) + (left + right)
                    store(i, c, own[c, at, :] * center[c, i] + lat[c, at, :] * around)
            if after:
                after(half // SUB)

    def into(buffer):
        def store(i, c, value):
            buffer[c, SUB + i * SUB : 2 * SUB + i * SUB, :] = value

        return store

    def enter(frame):
        for c in range(tiles_across):
            ping[c, SUB : SUB + rows, :] = frame[:, c * LANES : (c + 1) * LANES] * gain[c]

    enter(frame_ref)

    @pl.loop(0, count)
    def _(f):
        slot = f % 2

        @pl.when(f > 0)
        def _():
            load(f).wait()
            enter(loaded.at[f - 1])

        @pl.when(f + 1 < count)
        def _():
            @pl.when(f > 0)
            def _():
                load(f + 1).start()

        one_pass(ping, into(pong))
        one_pass(pong, into(ping))

        @pl.when(f >= 2)
        def _():
            for half in range(2):
                deliver(slot, f - 2, half).wait()

        def finish(i, c, value):
            tile, part = i * SUB // tile_rows, i * SUB % tile_rows
            ready[slot, tile * tiles_across + c, part : part + SUB, :] = value

        one_pass(ping, finish, lambda half: deliver(slot, f, half).start())

    for f in range(count - 2, count):
        for half in range(2):
            deliver(f % 2, f, half).wait()


def smooth(core, table, frames, frame, gain, mine, other, tiles_down, tile_rows, chips):
    count, height, width = frames.shape
    across = 2 * chips
    devices = tiles_down * across
    return pl.pallas_call(
        functools.partial(smooth_body, tiles_down, tile_rows, chips),
        out_shape=jax.ShapeDtypeStruct((devices, count * tile_rows, LANES), jnp.float32),
        in_specs=[pl.BlockSpec(memory_space=pltpu.SMEM)] * 2
        + [pl.BlockSpec(memory_space=pltpu.HBM)]
        + [pl.BlockSpec(memory_space=pltpu.VMEM)] * 4,
        out_specs=pl.BlockSpec(memory_space=pltpu.HBM),
        scratch_shapes=[pltpu.VMEM((count - 1, height, width), jnp.float32)]
        + [pltpu.VMEM((across, height, LANES), jnp.float32)] * 3
        + [pltpu.VMEM((across, height + 2 * SUB, LANES), jnp.float32)] * 2
        + [pltpu.VMEM((2, devices, tile_rows + SUB, LANES), jnp.float32)]
        + [pltpu.SemaphoreType.DMA((count - 1,)), pltpu.SemaphoreType.DMA((2, 2))],
        compiler_params=pltpu.CompilerParams(vmem_limit_bytes=50 << 20),
        name="smooth",
    )(core, table, frames, frame, gain, mine, other)


def convolve_body(count, rows, x_ref, high_ref, low_ref, out_ref, loaded, high, low, ready, load_sem, early_sem, late_sem):
    quarters, sources, pitch, _ = loaded.shape
    outputs = out_ref.shape[2]
    half = outputs // 2
    first, second = slice(0, half), slice(half, outputs)
    groups = rows // ROW_GROUP

    def load(q):
        part = pl.ds(q * sources, sources)
        return pltpu.make_async_copy(x_ref.at[part], loaded.at[q, :, 0 : count * rows, :], load_sem.at[q])

    def save(k, columns, sem):
        part = slice(k * ROW_GROUP, (k + 1) * ROW_GROUP)
        return pltpu.make_async_copy(ready.at[part, :, columns], out_ref.at[part, :, columns], sem.at[k])

    def prepare(q, k):
        flat = loaded.at[q].reshape(sources * pitch, LANES)
        for r in range(k * ROW_GROUP, (k + 1) * ROW_GROUP):
            parts = [flat[pl.ds(f * rows + r, sources, stride=pitch), :] for f in range(count)]
            x = jnp.concatenate(parts, axis=0).T
            top = x.astype(jnp.bfloat16)
            at = (slice(r * LANES, (r + 1) * LANES), slice(q * LANES, (q + 1) * LANES))
            high[at] = top
            low[at] = (x - top.astype(jnp.float32)).astype(jnp.bfloat16)

    def product(k, terms, columns):
        at = (slice(k * ROW_GROUP * LANES, (k + 1) * ROW_GROUP * LANES), terms)

        def dot(a_ref, b_ref):
            return jnp.dot(a_ref[at], b_ref[terms, columns], preferred_element_type=jnp.float32)

        result = dot(high, high_ref) + (dot(high, low_ref) + dot(low, high_ref))
        return result.reshape(ROW_GROUP, LANES, half)

    for q in range(quarters):
        load(q).start()
    load(0).wait()
    for k in range(groups):
        prepare(0, k)
    load(1).wait()
    prepare(1, 0)
    for k in range(groups):
        if k + 1 < groups:
            prepare(1, k + 1)
        else:
            load(2).wait()
            load(3).wait()
            prepare(2, 0)
            prepare(3, 0)
        ready[k * ROW_GROUP : (k + 1) * ROW_GROUP, :, first] = product(k, first, first)
        save(k, first, early_sem).start()
    for k in range(groups):
        if k + 1 < groups:
            prepare(2, k + 1)
            prepare(3, k + 1)
        ready[k * ROW_GROUP : (k + 1) * ROW_GROUP, :, second] = product(k, slice(0, outputs), second)
        save(k, second, late_sem).start()
    for k in range(groups):
        save(k, first, early_sem).wait()
        save(k, second, late_sem).wait()


def convolve(blocks, high, low, count, tile_rows):
    devices = blocks.shape[0]
    frames = high.shape[1]
    quarters = 4
    return pl.pallas_call(
        functools.partial(convolve_body, count, tile_rows),
        out_shape=jax.ShapeDtypeStruct((tile_rows, LANES, frames), jnp.float32),
        in_specs=[pl.BlockSpec(memory_space=pltpu.HBM)] + [pl.BlockSpec(memory_space=pltpu.VMEM)] * 2,
        out_specs=pl.BlockSpec(memory_space=pltpu.HBM),
        scratch_shapes=[pltpu.VMEM((quarters, devices // quarters, count * tile_rows + SUB, LANES), jnp.float32)]
        + [pltpu.VMEM((tile_rows * LANES, frames), jnp.bfloat16)] * 2
        + [pltpu.VMEM((tile_rows, LANES, frames), jnp.float32)]
        + [pltpu.SemaphoreType.DMA((quarters,))]
        + [pltpu.SemaphoreType.DMA((tile_rows // ROW_GROUP,))] * 2,
        compiler_params=pltpu.CompilerParams(vmem_limit_bytes=50 << 20),
        name="convolve",
    )(blocks, high, low)


def lookup(classes, mask, entry, count):
    result = jnp.zeros(classes.shape, jnp.float32)
    for k in range(count):
        result = jnp.where(classes == k, entry(k), result)
    return jnp.where(mask != 0, result, 0.0)


def lateral_body(class_ref, mask_ref, effusivity_ref, conductivity_ref, map_ref, table_ref, shared_ref):
    count = conductivity_ref.shape[0]
    rates = [lateral_rate * conductivity_ref[k] for k in range(count)]
    shared = jnp.int32(0)
    for k in range(count):
        table_ref[0, k] = rates[k]
        table_ref[1, k] = flux_factor * effusivity_ref[k]
        for other in range(k):
            shared = shared | (rates[k] == rates[other]).astype(jnp.int32)
    shared_ref[0] = shared
    lateral = lookup(class_ref[...], mask_ref[...], lambda k: rates[k], count)
    for peer in range(map_ref.shape[0]):
        map_ref[peer] = lateral


def lateral_for(peers, class_index, surface_mask, effusivity, conductivity):
    smem, vmem = pl.BlockSpec(memory_space=pltpu.SMEM), pl.BlockSpec(memory_space=pltpu.VMEM)
    return pl.pallas_call(
        lateral_body,
        out_shape=(
            jax.ShapeDtypeStruct((peers, *class_index.shape), jnp.float32),
            jax.ShapeDtypeStruct((2, conductivity.shape[0]), jnp.float32),
            jax.ShapeDtypeStruct((1,), jnp.int32),
        ),
        in_specs=[vmem, vmem, smem, smem],
        out_specs=(vmem, smem, smem),
        name="lateral",
    )(class_index, surface_mask, effusivity, conductivity)


def per_device(frames, class_index, surface_mask, effusivity, conductivity):
    tiles_down, chips = lax.axis_size("row"), lax.axis_size("chip")
    tile_rows = class_index.shape[0]
    count = frames.shape[0]
    devices = tiles_down * chips * 2
    core = lax.axis_index("core")

    peers = tiles_down * chips
    lateral, table, shared = lateral_for(peers, class_index, surface_mask, effusivity, conductivity)

    def smoothed(maps):
        mine = lax.all_to_all(maps, ("row", "chip"), split_axis=0, concat_axis=0, tiled=True)
        other = lax.ppermute(mine, "core", [(0, 1), (1, 0)])
        frame, gain = prime(table, frames, mine, tile_rows)
        number = core[None].astype(jnp.int32)
        return smooth(number, table, frames, frame, gain, mine, other, tiles_down, tile_rows, chips)

    def from_both():
        gain = lookup(class_index, surface_mask, lambda k: table[1, k], table.shape[1])
        return smoothed(jnp.concatenate([lateral, jnp.broadcast_to(gain[None], lateral.shape)], axis=1))

    blocks = lax.switch(shared[0], (lambda: smoothed(lateral), from_both))

    frame_ids = jnp.arange(devices * count, dtype=jnp.int32)
    quarter = devices // 4
    source = frame_ids // (quarter * count) * quarter + frame_ids % quarter
    arrival = source * count + frame_ids // quarter % count
    kernel = kernel_from(frame_ids, arrival).T
    rounded = lax.reduce_precision(kernel, 8, 7)
    high, low = rounded.astype(jnp.bfloat16), (kernel - rounded).astype(jnp.bfloat16)

    received = lax.all_to_all(blocks, ALL, split_axis=0, concat_axis=0, tiled=True)
    return convolve(received, high, low, count, tile_rows)


def solution(mesh):
    cores = Mesh(mesh.devices.reshape(mesh.shape["row"], mesh.shape["col"] // 2, 2), ALL)
    tile = P("row", ("chip", "core"))
    in_specs = (P(ALL, None, None), tile, tile, P(), P())
    return jax.shard_map(
        per_device, mesh=cores, in_specs=in_specs, out_specs=P("row", ("chip", "core"), None), check_vma=False
    )
```
